512 devices in a mesh: ctx: 64 (over z_hi, y, core), dp: 8 (over x, z_lo).
Axes of the slice: x: 4, y: 8, z: 8 (z_hi: 4, z_lo: 2; z = z_hi * 2 + z_lo), core: 2. Of those that a mesh axis runs over, the one named last changes fastest.
Arguments:
- tokens_in: bfloat16 [8, 8192, 8192], P('dp', 'ctx')
- queries_in: bfloat16 [8, 8192, 2048], P('dp', 'ctx'), may hold values from -6 to 6
- kv_weight: bfloat16 [8192, 256], P(('ctx', 'dp')), may hold values from -0.0625 to 0.0625
- out_grad: bfloat16 [8, 8192, 2048], P('dp', 'ctx'), may hold values from -6 to 6
- doc_lengths: int32 [8, 32], P('dp'), may hold values from 1 to 512, 8192 in all within a row
Outputs:
- attn_out: bfloat16 [8, 8192, 2048], P('dp', 'ctx')
- query_grad: bfloat16 [8, 8192, 2048], P('dp', 'ctx')
- weight_grad: float32 [8192, 256], P(('ctx', 'dp'))
The draws below stay inside these ranges and needn't reach their ends.
Inputs may be any that keep to these rules, and one draw needn't show every extreme that they name: `doc_lengths`: each row holds the lengths of the 32 documents of one sequence; they sum to 8192 and the longest is exactly 512.
All inputs are finite; a program needn't handle non-finite values.
Results may differ from the reference program's by a relative error of at most 0.034.
Values may be sent and summed in bfloat16 or wider, within the bound.
No kernel may reach another device: no remote copies, remote signals or barrier semaphores. Data moves between devices by JAX's collectives and lax.ppermute only.
A program may use at most 64 MiB of HBM per device.

```python
import math
import jax
import jax.numpy as jnp
import numpy as np
from jax import lax

D = 8192
HD = 128
G = 16
DOCS = 32
SEQ = 8192
MOST = 512
N_DP = 8


def draw_tokens_in(key, part):
    first_key = jax.random.fold_in(key, 0)
    base = jax.random.normal(first_key, (N_DP, SEQ, D), jnp.float32)
    base = jnp.clip(base, -6.0, 6.0)
    return base.astype(jnp.bfloat16)


def shard_levels(rng, shape, pieces, low, top_value):
    gain, own = 1.0, jax.random.fold_in(rng, 6)
    for position, shards_of in pieces:
        heights = jnp.exp(jax.random.uniform(jax.random.fold_in(own, position), (shards_of,), jnp.float32, low / len(pieces), top_value / len(pieces)))
        gain = gain * jnp.repeat(heights, shape[position] // shards_of).reshape([-1 if axis == position else 1 for axis in range(len(shape))])
    return gain


def split_up(count, total, most, lean):
    loads = [(1 << 20) // math.isqrt(grade ** lean) + 1 for grade in range(2, count + 1)]
    spare, counts = total - most - (count - 1), [1] * (count - 1)
    while spare > 0:
        candidates = [i for i in range(count - 1) if counts[i] < most]
        mass, remaining = sum([loads[i] for i in candidates]), spare
        for i in candidates:
            more = min(most - counts[i], max(1, remaining * loads[i] // mass), spare)
            counts[i] = counts[i] + more
            spare = spare - more
    return np.array([most] + counts)


def uneven(own_key, number_of, total, limit, skew):
    if number_of == 2:
        one = jax.random.randint(own_key, (), max(1, total - limit), min(limit, total - 1) + 1)
        return jnp.stack([one, total - one])
    lengths = jnp.asarray(split_up(number_of, total, limit, skew), jnp.int32)
    couples = (number_of - 1) // 2
    giver, receiver = lengths[1:1 + 2 * couples:2], lengths[2:2 + 2 * couples:2]
    room = jnp.minimum(giver - 1, limit - receiver)
    passed = jax.random.randint(jax.random.fold_in(own_key, 1), (couples,), 0, 1 << 20) % (room + 1)
    lengths = lengths.at[1:1 + 2 * couples:2].set(giver - passed).at[2:2 + 2 * couples:2].set(receiver + passed)
    return lengths[jax.random.permutation(jax.random.fold_in(own_key, 2), number_of)]


def gaussian(rng, extent, width, limit, shards=(), kind=jnp.bfloat16):
    array = width * jax.random.normal(rng, extent, jnp.float32)
    if shards:
        array = array * shard_levels(rng, extent, shards, -0.22, 0.18)
    return jnp.clip(array, -limit, limit).astype(kind)


def setup_inputs(seed: int = 0) -> dict:
    streams_of = jax.random.split(jax.random.key(seed), 6)
    tokens_in = draw_tokens_in(jax.random.fold_in(streams_of[5], 71), 0)
    queries_in = gaussian(streams_of[1], (N_DP, SEQ, G * HD), 1.0, 6.0, ((0, 8), (1, 64)))
    kv_weight = gaussian(streams_of[2], (D, 2 * HD), D ** -0.5, 0.0625, ((0, 512),))
    out_grad = gaussian(streams_of[3], (N_DP, SEQ, G * HD), 1.0, 6.0, ((0, 8), (1, 64)))
    doc_lengths = jax.vmap(lambda own: uneven(own, DOCS, SEQ, MOST, 2))(jax.random.split(streams_of[4], N_DP)).reshape((N_DP, DOCS)).astype(jnp.int32)
    return {"tokens_in": tokens_in, "queries_in": queries_in, "kv_weight": kv_weight, "out_grad": out_grad, "doc_lengths": doc_lengths}


def doc_index(positions, doc_ends):
    return jnp.sum((positions[:, None] >= doc_ends[None, :]).astype(jnp.int32), axis=1)


def rounded(values_in):
    return lax.optimization_barrier(values_in.astype(jnp.bfloat16)).astype(jnp.float32)


def reference(tokens_in, queries_in, kv_weight, out_grad, doc_lengths):
    qk_scale = HD ** -0.5
    block = math.gcd(SEQ, 512)
    n_blocks = SEQ // block
    window = block + MOST

    def one_seq(summed, inputs):
        local_in, query_all, grad_all, lens_in = inputs
        kv_rows = jnp.dot(local_in, kv_weight, preferred_element_type=jnp.float32).astype(jnp.bfloat16)
        padding = jnp.zeros((MOST, HD), jnp.bfloat16)
        key_pad = jnp.concatenate([padding, kv_rows[:, :HD]], axis=0)
        value_pad = jnp.concatenate([padding, kv_rows[:, HD:]], axis=0)
        doc_ends = jnp.cumsum(lens_in).astype(jnp.int32)

        def one_block(carry, block_idx):
            grad_k_pad, grad_v_pad = carry
            q_start = (block_idx * block).astype(jnp.int32)
            q_pos = q_start + jnp.arange(block, dtype=jnp.int32)
            k_pos = q_start - MOST + jnp.arange(window, dtype=jnp.int32)
            q_doc = doc_index(q_pos, doc_ends)
            k_doc = doc_index(k_pos, doc_ends)
            allowed = (k_pos[None, :] >= 0) & (k_pos[None, :] <= q_pos[:, None]) & (k_doc[None, :] == q_doc[:, None])
            mask3 = allowed[:, None, :]
            q_blk = lax.dynamic_slice_in_dim(query_all, q_start, block, 0).reshape(block, G, HD).astype(jnp.float32)
            d_blk = lax.dynamic_slice_in_dim(grad_all, q_start, block, 0).reshape(block, G, HD).astype(jnp.float32)
            k_blk = lax.dynamic_slice_in_dim(key_pad, q_start, window, 0).astype(jnp.float32)
            v_blk = lax.dynamic_slice_in_dim(value_pad, q_start, window, 0).astype(jnp.float32)
            scores = jnp.einsum("qgd,kd->qgk", q_blk, k_blk) * qk_scale
            row_max = jnp.max(jnp.where(mask3, scores, jnp.float32(-1e30)), axis=2)
            weights = jnp.where(mask3, jnp.exp(scores - row_max[:, :, None]), jnp.float32(0.0))
            row_sum = jnp.sum(weights, axis=2)
            attn = (jnp.einsum("qgk,kd->qgd", rounded(weights), v_blk) / row_sum[:, :, None]).astype(jnp.bfloat16)
            log_sum = row_max + jnp.log(row_sum)
            out_dot = jnp.sum(d_blk * attn.astype(jnp.float32), axis=2)
            probs = jnp.where(mask3, jnp.exp(scores - log_sum[:, :, None]), jnp.float32(0.0))
            dprobs = jnp.einsum("qgd,kd->qgk", d_blk, v_blk)
            dscores = rounded(probs * (dprobs - out_dot[:, :, None]))
            grad_q = (jnp.einsum("qgk,kd->qgd", dscores, k_blk) * qk_scale).astype(jnp.bfloat16)
            part_k = jnp.einsum("qgk,qgd->kd", dscores, q_blk) * qk_scale
            part_v = jnp.einsum("qgk,qgd->kd", rounded(probs), d_blk)
            old_k = lax.dynamic_slice_in_dim(grad_k_pad, q_start, window, 0)
            old_v = lax.dynamic_slice_in_dim(grad_v_pad, q_start, window, 0)
            grad_k_pad = lax.dynamic_update_slice_in_dim(grad_k_pad, old_k + part_k, q_start, 0)
            grad_v_pad = lax.dynamic_update_slice_in_dim(grad_v_pad, old_v + part_v, q_start, 0)
            return (grad_k_pad, grad_v_pad), (attn.reshape(block, G * HD), grad_q.reshape(block, G * HD))

        start_pad = (jnp.zeros((SEQ + MOST, HD), jnp.float32), jnp.zeros((SEQ + MOST, HD), jnp.float32))
        (grad_k_pad, grad_v_pad), (attn_blocks, grad_blocks) = lax.scan(one_block, start_pad, jnp.arange(n_blocks, dtype=jnp.int32))
        kv_grad = jnp.concatenate([grad_k_pad[MOST:], grad_v_pad[MOST:]], axis=1).astype(jnp.bfloat16)
        summed = summed + jnp.dot(local_in.T, kv_grad, preferred_element_type=jnp.float32)
        return summed, (attn_blocks.reshape(SEQ, G * HD), grad_blocks.reshape(SEQ, G * HD))

    start_sum = jnp.zeros((D, 2 * HD), jnp.float32)
    weight_grad, (attn_out, query_grad) = lax.scan(one_seq, start_sum, (tokens_in, queries_in, out_grad, doc_lengths))
    return attn_out, query_grad, weight_grad
```

```python
import jax
import jax.numpy as jnp
from jax import lax
from jax.sharding import Mesh, PartitionSpec as P

AXES = ("zh", "y", "core", "x", "zl")
CTX = ("zh", "y", "core")
DP = ("x", "zl")
TEAM = ("core", "x")
RING = ("zh", "y", "zl")


def exchanged(blocks, axes):
    return lax.all_to_all(blocks, axes, 0, 0, tiled=False)


def swapped(block):
    route = []
    for y in range(8):
        for x in range(4):
            hi, lo = divmod(y, 4)
            route.append((y * 4 + x, (hi * 4 + x) * 4 + lo))
    return lax.ppermute(block, ("y", "x"), route)


def shifted(block, hop):
    devices = range(64)
    return lax.ppermute(block, CTX, [(i, i + hop) for i in devices if i + hop in devices])


def doc_index(positions, doc_ends):
    return jnp.sum((positions[:, None] >= doc_ends[None, :]).astype(jnp.int32), axis=1)


def attention(queries, grads_out, keys, values, mask):
    scale = queries.shape[-1] ** -0.5
    mask3 = mask[:, None, :]
    scores = jnp.einsum("tgd,nd->tgn", queries, keys, preferred_element_type=jnp.float32) * scale
    top = jnp.max(jnp.where(mask3, scores, jnp.float32(-1e30)), axis=2, keepdims=True)
    weights = jnp.where(mask3, jnp.exp(scores - top), jnp.float32(0.0))
    total = jnp.sum(weights, axis=2, keepdims=True)
    attn = jnp.einsum("tgn,nd->tgd", weights.astype(jnp.bfloat16), values, preferred_element_type=jnp.float32)
    attn = (attn / total).astype(jnp.bfloat16)
    out_dot = jnp.sum(grads_out.astype(jnp.float32) * attn.astype(jnp.float32), axis=2, keepdims=True)
    probs = weights / total
    dprobs = jnp.einsum("tgd,nd->tgn", grads_out, values, preferred_element_type=jnp.float32)
    dscores = (probs * (dprobs - out_dot)).astype(jnp.bfloat16)
    grad_q = jnp.einsum("tgn,nd->tgd", dscores, keys, preferred_element_type=jnp.float32) * scale
    grad_k = jnp.einsum("tgn,tgd->nd", dscores, queries, preferred_element_type=jnp.float32) * scale
    grad_v = jnp.einsum("tgn,tgd->nd", probs.astype(jnp.bfloat16), grads_out, preferred_element_type=jnp.float32)
    return attn, grad_q.astype(jnp.bfloat16), jnp.concatenate([grad_k, grad_v], axis=1)


def per_device(tokens_in, queries_in, kv_weight, out_grad, doc_lengths):
    rows = tokens_in[0]
    count, features = rows.shape
    width = kv_weight.shape[1]
    head_dim = width // 2
    heads = queries_in.shape[2] // head_dim
    queries = queries_in[0].reshape(count, heads, head_dim)
    grads_out = out_grad[0].reshape(count, heads, head_dim)

    pieces = rows.reshape(count, 8, 4, 2, 128).transpose(3, 2, 0, 1, 4).reshape(8, count, features // 8)
    team_rows = exchanged(pieces, TEAM).reshape(8 * count, features // 8)
    held = swapped(kv_weight)
    weight = exchanged(jnp.broadcast_to(held[None], (64,) + held.shape), RING).reshape(features // 8, width)
    part = jnp.dot(team_rows, weight, preferred_element_type=jnp.float32)
    part = exchanged(part.astype(jnp.bfloat16).reshape(8, count, width), TEAM)
    kv = jnp.sum(part.astype(jnp.float32), axis=0).astype(jnp.bfloat16)

    doc_ends = jnp.cumsum(doc_lengths[0])
    first_pos = lax.axis_index(CTX) * count
    query_pos = first_pos + jnp.arange(count, dtype=jnp.int32)
    key_pos = first_pos - 4 * count + jnp.arange(5 * count, dtype=jnp.int32)
    mask = (
        (key_pos[None, :] >= 0)
        & (key_pos[None, :] <= query_pos[:, None])
        & (doc_index(key_pos, doc_ends)[None, :] == doc_index(query_pos, doc_ends)[:, None])
    )
    near = jnp.concatenate([shifted(kv, hop) for hop in (4, 3, 2, 1)] + [kv], axis=0)
    attn, query_grad, part_grad = attention(queries, grads_out, near[:, :head_dim], near[:, head_dim:], mask)
    kv_grad = part_grad[4 * count :]
    for hop in (1, 2, 3, 4):
        part = part_grad[(4 - hop) * count : (5 - hop) * count].astype(jnp.bfloat16)
        kv_grad = kv_grad + shifted(part, -hop).astype(jnp.float32)
    kv_grad = kv_grad.astype(jnp.bfloat16)

    team_grad = exchanged(jnp.broadcast_to(kv_grad[None], (8,) + kv_grad.shape), TEAM).reshape(8 * count, width)
    grad = lax.dot_general(team_rows, team_grad, (((0,), (0,)), ((), ())), preferred_element_type=jnp.float32)
    grad = exchanged(grad.astype(jnp.bfloat16).reshape(64, 16, width), RING)
    grad = jnp.sum(grad.astype(jnp.float32), axis=0)
    weight_grad = swapped(grad)
    shape = (1, count, heads * head_dim)
    return attn.reshape(shape), query_grad.reshape(shape), weight_grad


def solution(mesh):
    fine = Mesh(mesh.devices.reshape(4, 8, 2, 4, 2), AXES)
    return jax.shard_map(
        per_device,
        mesh=fine,
        in_specs=(P(DP, CTX, None), P(DP, CTX, None), P(AXES, None), P(DP, CTX, None), P(DP, None)),
        out_specs=(P(DP, CTX, None), P(DP, CTX, None), P(AXES, None)),
        check_vma=False,
    )
```

```python
import jax
import jax.numpy as jnp
from jax import lax
from jax.experimental import pallas as pl
from jax.experimental.pallas import tpu as pltpu
from jax.sharding import Mesh, PartitionSpec as P

AXES = ("zh", "y", "core", "x", "zl")
CTX = ("zh", "y", "core")
DP = ("x", "zl")
TEAM = ("core", "x")
RING = ("zh", "y", "zl")
ZH, Y, CORE, X, ZL = 4, 8, 2, 4, 2
MEMBERS = CORE * X
CHIPS = ZH * Y
COUNT = 128
HEAD = 128
WIDTH = 2 * HEAD
BF16, F32 = jnp.bfloat16, jnp.float32
VMEM_LIMIT = 40 << 20


def vmem():
    return pl.BlockSpec(memory_space=pltpu.VMEM)


def smem():
    return pl.BlockSpec(memory_space=pltpu.SMEM)


def params():
    return pltpu.CompilerParams(vmem_limit_bytes=VMEM_LIMIT)


def exchanged(blocks, axes):
    return lax.all_to_all(blocks, axes, 0, 0, tiled=False)


def target(core, x, step):
    return (core + step // X) % CORE, (x + step) % X


def source(core, x, step):
    return (core + step // X) % CORE, (x + X - step % X) % X


def to_team(piece, step):
    route = []
    for core in range(CORE):
        for x in range(X):
            to_core, to_x = target(core, x, step)
            route.append((core * X + x, to_core * X + to_x))
    return lax.ppermute(piece, TEAM, route)


def to_chip(block, hop):
    chips = range(CHIPS)
    return lax.ppermute(block, ("zh", "y"), [(i, i + hop) for i in chips if i + hop in chips])


def to_other_core(block):
    return lax.ppermute(block, "core", [(0, 1), (1, 0)])


def pieces_kernel(place, rows, *outs):
    group = pl.program_id(0)
    core, x = place[0], place[1]
    span = 32 * X
    for c in range(CORE):
        tiles = [rows[:, (b * CORE + c) * span : (b * CORE + c + 1) * span] for b in range(4)]
        for j in range(X):
            tile = jnp.concatenate([t[:, j * 32 : (j + 1) * 32] for t in tiles], axis=1)
            for step in range(MEMBERS):
                to_core, to_x = target(core, x, step)

                @pl.when((to_core == c) & (to_x == j))
                def _(step=step, tile=tile):
                    outs[step][...] = tile


def make_pieces(place, rows):
    features = rows.shape[1]
    groups = features // 1024
    return pl.pallas_call(
        pieces_kernel,
        grid_spec=pltpu.PrefetchScalarGridSpec(
            num_scalar_prefetch=1,
            grid=(groups,),
            in_specs=[pl.BlockSpec((COUNT, 1024), lambda i, s: (0, i))],
            out_specs=[pl.BlockSpec((COUNT, 128), lambda i, s: (0, i))] * MEMBERS,
        ),
        out_shape=[jax.ShapeDtypeStruct((COUNT, features // MEMBERS), BF16)] * MEMBERS,
        compiler_params=params(),
        cost_estimate=pl.CostEstimate(flops=0, bytes_accessed=4 << 20, transcendentals=0),
        name="pieces",
    )(place, rows)


def project_kernel(place, weight, *refs):
    pieces, out = refs[:MEMBERS], refs[MEMBERS]
    for step in range(MEMBERS):
        core, x = source(place[0], place[1], step)
        part = jnp.dot(pieces[step][...], weight[...], preferred_element_type=F32)
        out[core * X + x] = part.astype(BF16)


def project(place, weight, pieces):
    return pl.pallas_call(
        project_kernel,
        in_specs=[smem()] + [vmem()] * (1 + MEMBERS),
        out_specs=vmem(),
        out_shape=jax.ShapeDtypeStruct((MEMBERS, COUNT, WIDTH), BF16),
        compiler_params=params(),
        cost_estimate=pl.CostEstimate(flops=1 << 29, bytes_accessed=3 << 20, transcendentals=0),
        name="project",
    )(place, weight, *pieces)


def weight_grad_kernel(place, grads, *refs):
    pieces, out, total = refs[:MEMBERS], refs[MEMBERS], refs[MEMBERS + 1]
    turned, rows = [], []
    for step in range(MEMBERS):
        core, x = source(place[0], place[1], step)
        turned.append(grads[core * X + x].T)
        rows.append(pieces[step][...])
    total[...] = jnp.dot(
        jnp.concatenate(turned, axis=1), jnp.concatenate(rows, axis=0), preferred_element_type=F32
    )
    for chip in range(CHIPS):
        zh, y = divmod(chip, Y)
        if chip % 4 == 0:
            block = total[:, chip * 32 : chip * 32 + 128].T.astype(BF16)
        out[y, zh] = block[chip % 4 * 32 : chip % 4 * 32 + 32]


def weight_grad_parts(place, grads, pieces):
    features = pieces[0].shape[1]
    return pl.pallas_call(
        weight_grad_kernel,
        in_specs=[smem()] + [vmem()] * (1 + MEMBERS),
        out_specs=vmem(),
        out_shape=jax.ShapeDtypeStruct((Y, ZH, 32, WIDTH), BF16),
        scratch_shapes=[pltpu.VMEM((WIDTH, features), F32)],
        compiler_params=params(),
        cost_estimate=pl.CostEstimate(flops=1 << 29, bytes_accessed=3 << 20, transcendentals=0),
        name="weight_grad",
    )(place, grads, *pieces)


def attention_kernel(place, lengths, queries, grads, own, near, far, other, attn, grad_q, grad_own, grad_other):
    core, chip_pos = place[0], place[1]
    scale = HEAD ** -0.5
    blocks = [own[...], near[...], far[...], other[1 - core], other[2 - core]]
    starts = [chip_pos + core * COUNT - 2 * COUNT * i for i in range(3)]
    starts += [chip_pos + (1 - core) * COUNT - 2 * COUNT * (1 - core + i) for i in range(2)]
    keys = jnp.concatenate([b[:, :HEAD] for b in blocks], axis=0)
    values = jnp.concatenate([b[:, HEAD:] for b in blocks], axis=0)
    keys_t, values_t = keys.T, values.T

    query_pos = starts[0] + lax.broadcasted_iota(jnp.int32, (1, COUNT), 1)
    doc_start = jnp.zeros((1, COUNT), jnp.int32)
    end = jnp.int32(0)
    for doc in range(lengths.shape[1]):
        end = end + lengths[0, doc]
        doc_start = jnp.where(query_pos >= end, end, doc_start)
    row = lax.broadcasted_iota(jnp.int32, (COUNT, COUNT), 0)
    masks = []
    for start in starts:
        key_pos = start + row
        masks.append((key_pos >= doc_start) & (key_pos <= query_pos))
    mask = jnp.concatenate(masks, axis=0)
    mask = jnp.concatenate([mask, mask], axis=1)

    nt = (((1,), (1,)), ((), ()))
    total_k = total_v = None
    for pair in range(queries.shape[1] // WIDTH):
        cols = [slice((2 * pair + i) * HEAD, (2 * pair + i + 1) * HEAD) for i in range(2)]
        q = jnp.concatenate([queries[:, c] for c in cols], axis=0)
        g = jnp.concatenate([grads[:, c] for c in cols], axis=0)
        scores = lax.dot_general(keys, q, nt, preferred_element_type=F32) * scale
        scores = jnp.where(mask, scores, F32(-1e30))
        top = jnp.max(scores, axis=0, keepdims=True)
        weights = jnp.where(mask, jnp.exp(scores - top), F32(0.0))
        inverse = 1.0 / jnp.sum(weights, axis=0, keepdims=True)
        out = jnp.dot(values_t, weights.astype(BF16), preferred_element_type=F32) * inverse
        dprobs = lax.dot_general(values, g, nt, preferred_element_type=F32)
        probs = weights * inverse
        out_dot = jnp.sum(probs * dprobs, axis=0, keepdims=True)
        dscores = (probs * (dprobs - out_dot)).astype(BF16)
        dq = jnp.dot(keys_t, dscores, preferred_element_type=F32) * scale
        out, dq = out.T.astype(BF16), dq.T.astype(BF16)
        for i in range(2):
            attn[:, cols[i]] = out[i * COUNT : (i + 1) * COUNT]
            grad_q[:, cols[i]] = dq[i * COUNT : (i + 1) * COUNT]
        part_k = jnp.dot(dscores, q, preferred_element_type=F32)
        part_v = jnp.dot(probs.astype(BF16), g, preferred_element_type=F32)
        total_k = part_k if pair == 0 else total_k + part_k
        total_v = part_v if pair == 0 else total_v + part_v
    total = jnp.concatenate([total_k * scale, total_v], axis=1)
    for i in range(3):
        grad_own[i] = total[i * COUNT : (i + 1) * COUNT]
    for i in range(2):
        grad_other[i] = total[(3 + i) * COUNT : (4 + i) * COUNT].astype(BF16)


def attention(place, lengths, queries, grads, own, near, far, other):
    shape = jax.ShapeDtypeStruct(queries.shape, BF16)
    return pl.pallas_call(
        attention_kernel,
        in_specs=[smem(), smem()] + [vmem()] * 6,
        out_specs=[vmem()] * 4,
        out_shape=[
            shape,
            shape,
            jax.ShapeDtypeStruct((3, COUNT, WIDTH), F32),
            jax.ShapeDtypeStruct((2, COUNT, WIDTH), BF16),
        ],
        compiler_params=params(),
        cost_estimate=pl.CostEstimate(flops=2 << 30, bytes_accessed=3 << 20, transcendentals=5 << 18),
        name="attention",
    )(place, lengths, queries, grads, own, near, far, other)


def per_device(tokens_in, queries_in, kv_weight, out_grad, doc_lengths):
    core = lax.axis_index("core")
    chip = lax.axis_index(("zh", "y"))
    team_place = jnp.stack([core, lax.axis_index("x")]).astype(jnp.int32)
    ctx_place = jnp.stack([core, chip * (CORE * COUNT)]).astype(jnp.int32)
    ring = ZH * Y * ZL

    weight = exchanged(jnp.broadcast_to(kv_weight[None], (ring,) + kv_weight.shape), RING)
    weight = weight.reshape(ring * kv_weight.shape[0], WIDTH)
    pieces = make_pieces(team_place, tokens_in[0])
    pieces = [pieces[0]] + [to_team(pieces[step], step) for step in range(1, MEMBERS)]
    part = exchanged(project(team_place, weight, pieces), TEAM)
    kv = jnp.sum(part.astype(F32), axis=0).astype(BF16)

    near, far = to_chip(kv, 1), to_chip(kv, 2)
    other = to_other_core(jnp.stack([kv, near, far]))
    attn, query_grad, grad_own, grad_other = attention(
        ctx_place, doc_lengths, queries_in[0], out_grad[0], kv, near, far, other
    )

    back = to_other_core(grad_other).astype(F32)
    first = core == 0
    far_grad = grad_own[2] + jnp.where(first, F32(0.0), back[1])
    near_grad = grad_own[1] + jnp.where(first, back[1], back[0])
    own_grad = grad_own[0] + jnp.where(first, back[0], F32(0.0))
    far_grad, near_grad = to_chip(far_grad.astype(BF16), -2), to_chip(near_grad.astype(BF16), -1)
    kv_grad = (own_grad + near_grad.astype(F32) + far_grad.astype(F32)).astype(BF16)

    team_grad = exchanged(jnp.broadcast_to(kv_grad[None], (MEMBERS,) + kv_grad.shape), TEAM)
    parts = weight_grad_parts(team_place, team_grad, pieces)
    parts = jnp.sum(exchanged(parts, "y").astype(F32), axis=0).astype(BF16)
    parts = exchanged(parts.reshape(ZH * ZL, 16, WIDTH), ("zh", "zl"))
    weight_grad = jnp.sum(parts.astype(F32), axis=0)
    return attn[None], query_grad[None], weight_grad


def solution(mesh):
    fine = Mesh(mesh.devices.reshape(ZH, Y, CORE, X, ZL), AXES)
    return jax.shard_map(
        per_device,
        mesh=fine,
        in_specs=(P(DP, CTX, None), P(DP, CTX, None), P(AXES, None), P(DP, CTX, None), P(DP, None)),
        out_specs=(P(DP, CTX, None), P(DP, CTX, None), P(AXES, None)),
        check_vma=False,
    )
```

```python
import functools

import jax
import jax.numpy as jnp
from jax import lax
from jax.experimental import pallas as pl
from jax.experimental.pallas import tpu as pltpu
from jax.sharding import Mesh, PartitionSpec as P

AXES = ("zh", "y", "core", "x", "zl")
CTX = ("zh", "y", "core")
DP = ("x", "zl")
ZH, Y, CORE, X, ZL = 4, 8, 2, 4, 2
CHIPS = ZH * Y
COUNT = 128
HEAD = 128
WIDTH = 2 * HEAD
BF16, F32 = jnp.bfloat16, jnp.float32
LOG2E = 1.4426950408889634
VMEM_LIMIT = 40 << 20


def vmem():
    return pl.BlockSpec(memory_space=pltpu.VMEM)


def smem():
    return pl.BlockSpec(memory_space=pltpu.SMEM)


def params():
    return pltpu.CompilerParams(vmem_limit_bytes=VMEM_LIMIT)


def exchanged(blocks, axes):
    return lax.all_to_all(blocks, axes, 0, 0, tiled=False)


def to_team(piece, step):
    return lax.ppermute(piece, "x", [(x, (x + step) % X) for x in range(X)])


def to_chip(block, hop):
    chips = range(CHIPS)
    return lax.ppermute(block, ("zh", "y"), [(i, i + hop) for i in chips if i + hop in chips])


def to_other_core(block):
    return lax.ppermute(block, "core", [(0, 1), (1, 0)])


def pieces_kernel(place, rows, own, ahead, behind, over, under, sorted_rows):
    core, x = place[0], place[1]
    span = 32 * X
    old = lax.broadcasted_iota(jnp.int32, (4 * span, 4 * span), 0)
    new = lax.broadcasted_iota(jnp.int32, (4 * span, 4 * span), 1)
    moved = (old // 32 % X) * span + (old // span) * 32 + old % 32
    turn = (new == moved).astype(F32).astype(BF16)
    for group in range(CHIPS // 4):
        for c in range(CORE):
            tiles = [rows[:, ((group * 4 + b) * CORE + c) * span :][:, :span] for b in range(4)]
            tile = jnp.dot(jnp.concatenate(tiles, axis=1), turn, preferred_element_type=F32).astype(BF16)
            for j in range(X):
                sorted_rows[c * X + j, :, group * span : (group + 1) * span] = tile[:, j * span : (j + 1) * span]
    for half in range(2):
        first = (core + half) % CORE * X
        own[half] = sorted_rows[first + x]
        ahead[half] = sorted_rows[first + (x + 1) % X]
        behind[half] = sorted_rows[first + (x + 3) % X]
        (over, under)[half][...] = sorted_rows[first + (x + 2) % X]


def make_pieces(place, rows):
    features = rows.shape[1] // (CORE * X)
    piece = (COUNT, features)
    return pl.pallas_call(
        pieces_kernel,
        in_specs=[smem(), vmem()],
        out_specs=[vmem()] * 5,
        out_shape=[jax.ShapeDtypeStruct(shape, BF16) for shape in [(2,) + piece] * 3 + [piece] * 2],
        scratch_shapes=[
            pltpu.VMEM((CORE * X,) + piece, BF16),
        ],
        compiler_params=params(),
        cost_estimate=pl.CostEstimate(flops=1 << 30, bytes_accessed=4 << 20, transcendentals=0),
        name="pieces",
    )(place, rows)


def team_pieces(own, ahead, behind, over, under):
    halfway = to_team(over, 1), to_team(under, -1)
    pieces = own, to_team(behind, -1), to_team(ahead, 1), to_team(halfway[0], 1), to_team(halfway[1], -1)
    return pieces, halfway


def halves(refs, half):
    own, after, before, over, under = refs
    return [(0, own[half]), (1, after[half]), (3, before[half]), (2, (over, under)[half][...])]


def project_kernel(place, weight, weight_other, own, after, before, over, under, out):
    refs = (own, after, before, over, under)
    rows = [w[...].reshape(ZH * Y * 32, WIDTH) for w in (weight, weight_other)]
    for (step, first), (_, second) in zip(halves(refs, 0), halves(refs, 1)):
        part = jnp.dot(first, rows[0], preferred_element_type=F32)
        part += jnp.dot(second, rows[1], preferred_element_type=F32)
        out[(place[1] + step) % X] = part.astype(BF16)


def project(place, weight, weight_other, pieces):
    return pl.pallas_call(
        project_kernel,
        in_specs=[smem()] + [vmem()] * 7,
        out_specs=vmem(),
        out_shape=jax.ShapeDtypeStruct((X, COUNT, WIDTH), BF16),
        compiler_params=params(),
        cost_estimate=pl.CostEstimate(flops=1 << 29, bytes_accessed=3 << 20, transcendentals=0),
        name="project",
    )(place, weight, weight_other, *pieces)


def weight_grad_kernel(half, place, grads, own, after, before, over, under, out, total):
    turned, rows = [], []
    for step, piece in halves((own, after, before, over, under), half):
        turned.append(grads[(place[1] + step) % X].T)
        rows.append(piece)
    total[...] = jnp.dot(
        jnp.concatenate(turned, axis=1), jnp.concatenate(rows, axis=0), preferred_element_type=F32
    )
    for four in range(CHIPS // 4):
        block = total[:, four * 128 : four * 128 + 128].T
        for i in range(4):
            zh, y = divmod(four * 4 + i, Y)
            out[y, zh] = block[i * 32 : i * 32 + 32].astype(BF16)


def weight_grad_parts(half, place, grads, pieces):
    features = pieces[0].shape[2]
    return pl.pallas_call(
        functools.partial(weight_grad_kernel, half),
        in_specs=[smem()] + [vmem()] * 6,
        out_specs=vmem(),
        out_shape=jax.ShapeDtypeStruct((Y, ZH, 32, WIDTH), BF16),
        scratch_shapes=[pltpu.VMEM((WIDTH, features), F32)],
        compiler_params=params(),
        cost_estimate=pl.CostEstimate(flops=1 << 28, bytes_accessed=2 << 20, transcendentals=0),
        name="weight_grad",
    )(place, grads, *pieces)


def summed_kernel(parts, out):
    total = parts[0].astype(F32)
    for i in range(1, parts.shape[0]):
        total = total + parts[i].astype(F32)
    out[...] = total.astype(out.dtype)


def summed(parts, kind):
    return pl.pallas_call(
        summed_kernel,
        in_specs=[vmem()],
        out_specs=vmem(),
        out_shape=jax.ShapeDtypeStruct(parts.shape[1:], kind),
        compiler_params=params(),
        name="summed",
    )(parts)


def attention_kernel(place, lengths, queries, grads, own, near, far, other, attn, grad_q, grad_own, grad_other):
    core, chip_pos = place[0], place[1]
    scale = HEAD ** -0.5
    blocks = [own[...], near[...], far[...], other[1 - core], other[2 - core]]
    starts = [chip_pos + core * COUNT - 2 * COUNT * i for i in range(3)]
    starts += [chip_pos + (1 - core) * COUNT - 2 * COUNT * (1 - core + i) for i in range(2)]
    keys = jnp.concatenate([b[:, :HEAD] for b in blocks], axis=0)
    values = jnp.concatenate([b[:, HEAD:] for b in blocks], axis=0)
    keys_t, values_t = keys.T, values.T

    query_pos = starts[0] + lax.broadcasted_iota(jnp.int32, (1, COUNT), 1)
    doc_start = jnp.zeros((1, COUNT), jnp.int32)
    end = jnp.int32(0)
    for doc in range(lengths.shape[1]):
        end = end + lengths[0, doc]
        doc_start = jnp.where(query_pos >= end, end, doc_start)
    row = lax.broadcasted_iota(jnp.int32, (COUNT, COUNT), 0)
    masks = []
    for start in starts:
        key_pos = start + row
        masks.append((key_pos >= doc_start) & (key_pos <= query_pos))
    cap = jnp.where(jnp.concatenate(masks, axis=0), F32(jnp.inf), F32(-1e30))
    cap = jnp.concatenate([cap, cap], axis=1)

    nt = (((1,), (1,)), ((), ()))
    total_k = total_v = None
    for pair in range(queries.shape[1] // WIDTH):
        cols = [slice((2 * pair + i) * HEAD, (2 * pair + i + 1) * HEAD) for i in range(2)]
        q = jnp.concatenate([queries[:, c] for c in cols], axis=0)
        g = jnp.concatenate([grads[:, c] for c in cols], axis=0)
        scores = lax.dot_general(keys, q, nt, preferred_element_type=F32) * F32(scale * LOG2E)
        scores = jnp.minimum(scores, cap)
        top = jnp.max(scores, axis=0, keepdims=True)
        weights = jnp.exp2(scores - top)
        inverse = 1.0 / jnp.sum(weights, axis=0, keepdims=True)
        dprobs = lax.dot_general(values, g, nt, preferred_element_type=F32)
        out_dot = jnp.sum(weights * dprobs, axis=0, keepdims=True) * inverse
        dscores = (weights * (dprobs - out_dot)).astype(BF16)
        weights = weights.astype(BF16)
        out = jnp.dot(values_t, weights, preferred_element_type=F32) * inverse
        dq = jnp.dot(keys_t, dscores, preferred_element_type=F32) * (inverse * scale)
        out, dq = out.T.astype(BF16), dq.T.astype(BF16)
        for i in range(2):
            attn[:, cols[i]] = out[i * COUNT : (i + 1) * COUNT]
            grad_q[:, cols[i]] = dq[i * COUNT : (i + 1) * COUNT]
        column = jnp.broadcast_to(inverse, (HEAD, WIDTH)).T
        part_k = jnp.dot(dscores, (q.astype(F32) * column).astype(BF16), preferred_element_type=F32)
        part_v = jnp.dot(weights, (g.astype(F32) * column).astype(BF16), preferred_element_type=F32)
        total_k = part_k if pair == 0 else total_k + part_k
        total_v = part_v if pair == 0 else total_v + part_v
    total = jnp.concatenate([total_k * scale, total_v], axis=1)
    for i in range(3):
        grad_own[i] = total[i * COUNT : (i + 1) * COUNT]
    for i in range(2):
        grad_other[i] = total[(3 + i) * COUNT : (4 + i) * COUNT].astype(BF16)


def attention(place, lengths, queries, grads, own, near, far, other):
    shape = jax.ShapeDtypeStruct(queries.shape, BF16)
    return pl.pallas_call(
        attention_kernel,
        in_specs=[smem(), smem()] + [vmem()] * 6,
        out_specs=[vmem()] * 4,
        out_shape=[
            shape,
            shape,
            jax.ShapeDtypeStruct((3, COUNT, WIDTH), F32),
            jax.ShapeDtypeStruct((2, COUNT, WIDTH), BF16),
        ],
        compiler_params=params(),
        cost_estimate=pl.CostEstimate(flops=2 << 30, bytes_accessed=3 << 20, transcendentals=5 << 18),
        name="attention",
    )(place, lengths, queries, grads, own, near, far, other)


def per_device(tokens_in, queries_in, kv_weight, out_grad, doc_lengths):
    core = lax.axis_index("core")
    chip = lax.axis_index(("zh", "y"))
    team_place = jnp.stack([core, lax.axis_index("x")]).astype(jnp.int32)
    ctx_place = jnp.stack([core, chip * (CORE * COUNT)]).astype(jnp.int32)

    pieces = make_pieces(team_place, tokens_in[0])
    ring = ZH * Y * ZL
    weight = exchanged(jnp.broadcast_to(kv_weight[None], (ring,) + kv_weight.shape), ("zh", "y", "zl"))
    pieces, halfway = team_pieces(*pieces)
    weight, _ = lax.optimization_barrier((weight, halfway))
    weight_other = to_other_core(weight)
    part = exchanged(project(team_place, weight, weight_other, pieces), "x")
    kv = summed(part, BF16)

    near, far = to_chip(kv, 1), to_chip(kv, 2)
    other = to_other_core(jnp.stack([kv, near, far]))
    attn, query_grad, grad_own, grad_other = attention(
        ctx_place, doc_lengths, queries_in[0], out_grad[0], kv, near, far, other
    )

    back = to_other_core(grad_other).astype(F32)
    first = core == 0
    far_grad = grad_own[2] + jnp.where(first, F32(0.0), back[1])
    near_grad = grad_own[1] + jnp.where(first, back[1], back[0])
    own_grad = grad_own[0] + jnp.where(first, back[0], F32(0.0))
    far_grad, near_grad = to_chip(far_grad.astype(BF16), -2), to_chip(near_grad.astype(BF16), -1)
    kv_grad = (own_grad + near_grad.astype(F32) + far_grad.astype(F32)).astype(BF16)

    team_grad = exchanged(jnp.broadcast_to(kv_grad[None], (X,) + kv_grad.shape), "x")
    theirs = to_other_core(weight_grad_parts(1, team_place, team_grad, pieces))
    ours = weight_grad_parts(0, team_place, team_grad, pieces)
    parts = exchanged((ours.astype(F32) + theirs.astype(F32)).astype(BF16), "y")
    parts = summed(parts, BF16).reshape(ZH * ZL, 16, WIDTH)
    weight_grad = summed(exchanged(parts, ("zh", "zl")), F32)
    return attn[None], query_grad[None], weight_grad


def solution(mesh):
    fine = Mesh(mesh.devices.reshape(ZH, Y, CORE, X, ZL), AXES)
    return jax.shard_map(
        per_device,
        mesh=fine,
        in_specs=(P(DP, CTX, None), P(DP, CTX, None), P(AXES, None), P(DP, CTX, None), P(DP, None)),
        out_specs=(P(DP, CTX, None), P(DP, CTX, None), P(AXES, None)),
        check_vma=False,
    )
```

```python
import functools

import jax
import jax.numpy as jnp
from jax import lax
from jax.experimental import pallas as pl
from jax.experimental.pallas import tpu as pltpu
from jax.sharding import Mesh, PartitionSpec as P

AXES = ("zh", "yh", "yl", "core", "x", "zl")
CTX = ("zh", "yh", "yl", "core")
CHIP = ("zh", "yh", "yl")
DP = ("x", "zl")
ZH, YH, YL, CORE, X, ZL = 4, 4, 2, 2, 4, 2
CHIPS = ZH * YH * YL
COUNT = 128
HEAD = 128
WIDTH = 2 * HEAD
BF16, F32 = jnp.bfloat16, jnp.float32
TOGETHER = 8
LOG2E = 1.4426950408889634
VMEM_LIMIT = 20 << 20
SMALL_LIMIT = 8 << 20


def vmem():
    return pl.BlockSpec(memory_space=pltpu.VMEM)


def smem():
    return pl.BlockSpec(memory_space=pltpu.SMEM)


def params(limit=VMEM_LIMIT):
    return pltpu.CompilerParams(vmem_limit_bytes=limit)


def small_call(kernel, *args, outs, name, places=0):
    return pl.pallas_call(
        kernel,
        in_specs=[smem()] * places + [vmem()] * (len(args) - places),
        out_specs=[vmem()] * len(outs),
        out_shape=[jax.ShapeDtypeStruct(shape, kind) for shape, kind in outs],
        compiler_params=params(SMALL_LIMIT),
        cost_estimate=pl.CostEstimate(flops=1 << 18, bytes_accessed=1 << 19, transcendentals=0),
        name=name,
    )(*args)


def exchanged(blocks, axes):
    return lax.all_to_all(blocks, axes, 0, 0, tiled=False)


def to_team(piece, step):
    return lax.ppermute(piece, "x", [(x, (x + step) % X) for x in range(X)])


def to_chip(block, hop):
    chips = range(CHIPS)
    return lax.ppermute(block, CHIP, [(i, i + hop) for i in chips if i + hop in chips])


def to_other_core(block):
    return lax.ppermute(block, "core", [(0, 1), (1, 0)])


def pieces_kernel(place, rows, own, ahead, behind, over, under, sorted_rows):
    core, x = place[0], place[1]
    span = 32 * X
    old = lax.broadcasted_iota(jnp.int32, (4 * span, 4 * span), 0)
    new = lax.broadcasted_iota(jnp.int32, (4 * span, 4 * span), 1)
    moved = (old // 32 % X) * span + (old // span) * 32 + old % 32
    turn = (new == moved).astype(F32).astype(BF16)
    for group in range(CHIPS // 4):
        for c in range(CORE):
            tiles = [rows[:, ((group * 4 + b) * CORE + c) * span :][:, :span] for b in range(4)]
            tile = jnp.dot(jnp.concatenate(tiles, axis=1), turn, preferred_element_type=F32).astype(BF16)
            for j in range(X):
                sorted_rows[c * X + j, :, group * span : (group + 1) * span] = tile[:, j * span : (j + 1) * span]
    for half in range(2):
        first = (core + half) % CORE * X
        own[half] = sorted_rows[first + x]
        ahead[half] = sorted_rows[first + (x + 1) % X]
        behind[half] = sorted_rows[first + (x + 3) % X]
        (over, under)[half][...] = sorted_rows[first + (x + 2) % X]


def make_pieces(place, rows):
    features = rows.shape[1] // (CORE * X)
    piece = (COUNT, features)
    return pl.pallas_call(
        pieces_kernel,
        in_specs=[smem(), vmem()],
        out_specs=[vmem()] * 5,
        out_shape=[jax.ShapeDtypeStruct(shape, BF16) for shape in [(2,) + piece] * 3 + [piece] * 2],
        scratch_shapes=[
            pltpu.VMEM((CORE * X,) + piece, BF16),
        ],
        compiler_params=params(),
        cost_estimate=pl.CostEstimate(flops=1 << 30, bytes_accessed=4 << 20, transcendentals=0),
        name="pieces",
    )(place, rows)


def team_pieces(own, ahead, behind, over, under):
    halfway = to_team(over, 1), to_team(under, -1)
    pieces = own, to_team(behind, -1), to_team(ahead, 1), to_team(halfway[0], 1), to_team(halfway[1], -1)
    return pieces, halfway


def halves(refs, half):
    own, after, before, over, under = refs
    return [(0, own[half]), (1, after[half]), (3, before[half]), (2, (over, under)[half][...])]


def project_kernel(place, weight, weight_other, own, after, before, over, under, early_q, early_g, out):
    del early_q, early_g
    refs = (own, after, before, over, under)
    rows = [w[...].reshape(CHIPS * 32, WIDTH) for w in (weight, weight_other)]
    for (step, first), (_, second) in zip(halves(refs, 0), halves(refs, 1)):
        part = jnp.dot(first, rows[0], preferred_element_type=F32)
        part += jnp.dot(second, rows[1], preferred_element_type=F32)
        out[(place[1] + step) % X] = part.astype(BF16)


def project(place, weight, weight_other, pieces, *early):
    return pl.pallas_call(
        project_kernel,
        in_specs=[smem()] + [vmem()] * 9,
        out_specs=vmem(),
        out_shape=jax.ShapeDtypeStruct((X, COUNT, WIDTH), BF16),
        compiler_params=params(),
        cost_estimate=pl.CostEstimate(flops=1 << 29, bytes_accessed=3 << 20, transcendentals=0),
        name="project",
    )(place, weight, weight_other, *pieces, *early)


def weight_grad_kernel(half, place, grads, own, after, before, over, under, out, total):
    turned, rows = [], []
    for step, piece in halves((own, after, before, over, under), half):
        turned.append(grads[(place[1] + step) % X].T)
        rows.append(piece)
    total[...] = jnp.dot(
        jnp.concatenate(turned, axis=1), jnp.concatenate(rows, axis=0), preferred_element_type=F32
    )
    for four in range(CHIPS // 4):
        block = total[:, four * 128 : four * 128 + 128].T.astype(BF16)
        for i in range(4):
            far, yl = divmod(four * 4 + i, YL)
            for zl in range(ZL):
                row = i * 32 + zl * 16
                out[yl * ZL + zl, far] = block[row : row + 16]


def weight_grad_parts(half, place, grads, pieces):
    features = pieces[0].shape[2]
    return pl.pallas_call(
        functools.partial(weight_grad_kernel, half),
        in_specs=[smem()] + [vmem()] * 6,
        out_specs=vmem(),
        out_shape=jax.ShapeDtypeStruct((YL * ZL, ZH * YH, 16, WIDTH), BF16),
        scratch_shapes=[pltpu.VMEM((WIDTH, features), F32)],
        compiler_params=params(),
        cost_estimate=pl.CostEstimate(flops=1 << 28, bytes_accessed=2 << 20, transcendentals=0),
        name="weight_grad",
    )(place, grads, *pieces)


def summed_kernel(parts, out):
    total = parts[0].astype(F32)
    for i in range(1, parts.shape[0]):
        total = total + parts[i].astype(F32)
    out[...] = total.astype(out.dtype)


def summed(parts, kind):
    return small_call(summed_kernel, parts, outs=[(parts.shape[1:], kind)], name="summed")[0]


def spread_kernel(block, out):
    for i in range(out.shape[0]):
        out[i] = block[...]


def spread(block, count):
    return small_call(spread_kernel, block, outs=[((count,) + block.shape, block.dtype)], name="spread")[0]


def stacked_kernel(*refs):
    for i, block in enumerate(refs[:-1]):
        refs[-1][i] = block[...]


def stacked(*blocks):
    shape = (len(blocks),) + blocks[0].shape
    return small_call(stacked_kernel, *blocks, outs=[(shape, blocks[0].dtype)], name="stacked")[0]


def added_kernel(one, other, out):
    out[...] = (one[...].astype(F32) + other[...].astype(F32)).astype(BF16)


def added(one, other):
    return small_call(added_kernel, one, other, outs=[(one.shape, BF16)], name="added")[0]


def homeward_kernel(place, own, back, total_own, near, far):
    first = place[0] == 0
    zero, one = back[0].astype(F32), back[1].astype(F32)
    total_own[...] = own[0] + jnp.where(first, zero, F32(0.0))
    near[...] = (own[1] + jnp.where(first, one, zero)).astype(BF16)
    far[...] = (own[2] + jnp.where(first, F32(0.0), one)).astype(BF16)


def homeward(place, own, back):
    block = own.shape[1:]
    outs = [(block, F32), (block, BF16), (block, BF16)]
    return small_call(homeward_kernel, place, own, back, outs=outs, name="homeward", places=1)


def gathered_kernel(own, near, far, out):
    total = (own[...] + near[...].astype(F32) + far[...].astype(F32)).astype(BF16)
    for i in range(out.shape[0]):
        out[i] = total


def gathered(own, near, far, count):
    return small_call(gathered_kernel, own, near, far, outs=[((count,) + own.shape, BF16)], name="gathered")[0]


def attention_kernel(place, lengths, queries, grads, own, near, far, other, attn, grad_q, grad_own, grad_other):
    core, chip_pos = place[0], place[2]
    scale = HEAD ** -0.5
    blocks = [own[...], near[...], far[...], other[1 - core], other[2 - core]]
    starts = [chip_pos + core * COUNT - 2 * COUNT * i for i in range(3)]
    starts += [chip_pos + (1 - core) * COUNT - 2 * COUNT * (1 - core + i) for i in range(2)]
    keys = jnp.concatenate([b[:, :HEAD] for b in blocks], axis=0)
    values = jnp.concatenate([b[:, HEAD:] for b in blocks], axis=0)
    keys_t, values_t = keys.T, values.T

    query_pos = starts[0] + lax.broadcasted_iota(jnp.int32, (1, COUNT), 1)
    doc_start = jnp.zeros((1, COUNT), jnp.int32)
    end = jnp.int32(0)
    for doc in range(lengths.shape[1]):
        end = end + lengths[0, doc]
        doc_start = jnp.where(query_pos >= end, end, doc_start)
    row = lax.broadcasted_iota(jnp.int32, (COUNT, COUNT), 0)
    masks = []
    for start in starts:
        key_pos = start + row
        masks.append((key_pos >= doc_start) & (key_pos <= query_pos))
    cap = jnp.where(jnp.concatenate(masks, axis=0), F32(jnp.inf), F32(-1e30))
    cap = jnp.concatenate([cap] * TOGETHER, axis=1)

    nt = (((1,), (1,)), ((), ()))
    total_k = total_v = None
    for turn in range(queries.shape[1] // (TOGETHER * HEAD)):
        cols = [slice(h * HEAD, (h + 1) * HEAD) for h in range(turn * TOGETHER, (turn + 1) * TOGETHER)]
        q = jnp.concatenate([queries[:, c] for c in cols], axis=0)
        g = jnp.concatenate([grads[:, c] for c in cols], axis=0)
        scores = lax.dot_general(keys, q, nt, preferred_element_type=F32) * F32(scale * LOG2E)
        scores = jnp.minimum(scores, cap)
        top = jnp.max(scores, axis=0, keepdims=True)
        weights = jnp.exp2(scores - top)
        inverse = 1.0 / jnp.sum(weights, axis=0, keepdims=True)
        dprobs = lax.dot_general(values, g, nt, preferred_element_type=F32)
        out_dot = jnp.sum(weights * dprobs, axis=0, keepdims=True) * inverse
        dscores = (weights * (dprobs - out_dot)).astype(BF16)
        weights = weights.astype(BF16)
        out = jnp.dot(values_t, weights, preferred_element_type=F32) * inverse
        dq = jnp.dot(keys_t, dscores, preferred_element_type=F32) * (inverse * scale)
        out, dq = out.T.astype(BF16), dq.T.astype(BF16)
        for i in range(TOGETHER):
            attn[:, cols[i]] = out[i * COUNT : (i + 1) * COUNT]
            grad_q[:, cols[i]] = dq[i * COUNT : (i + 1) * COUNT]
        column = jnp.broadcast_to(inverse, (HEAD, TOGETHER * HEAD)).T
        part_k = jnp.dot(dscores, (q.astype(F32) * column).astype(BF16), preferred_element_type=F32)
        part_v = jnp.dot(weights, (g.astype(F32) * column).astype(BF16), preferred_element_type=F32)
        total_k = part_k if turn == 0 else total_k + part_k
        total_v = part_v if turn == 0 else total_v + part_v
    total = jnp.concatenate([total_k * scale, total_v], axis=1)
    for i in range(3):
        grad_own[i] = total[i * COUNT : (i + 1) * COUNT]
    for i in range(2):
        grad_other[i] = total[(3 + i) * COUNT : (4 + i) * COUNT].astype(BF16)


def attention(place, lengths, queries, grads, own, near, far, other):
    shape = jax.ShapeDtypeStruct(queries.shape, BF16)
    return pl.pallas_call(
        attention_kernel,
        in_specs=[smem(), smem()] + [vmem()] * 6,
        out_specs=[vmem()] * 4,
        out_shape=[
            shape,
            shape,
            jax.ShapeDtypeStruct((3, COUNT, WIDTH), F32),
            jax.ShapeDtypeStruct((2, COUNT, WIDTH), BF16),
        ],
        compiler_params=params(),
        cost_estimate=pl.CostEstimate(flops=2 << 30, bytes_accessed=3 << 20, transcendentals=5 << 18),
        name="attention",
    )(place, lengths, queries, grads, own, near, far, other)


def per_device(tokens_in, queries_in, kv_weight, out_grad, doc_lengths):
    core, chip = lax.axis_index("core"), lax.axis_index(CHIP)
    place = jnp.stack([core, lax.axis_index("x"), chip * (CORE * COUNT)]).astype(jnp.int32)

    cut = make_pieces(place, tokens_in[0])
    ring = CHIPS * ZL
    weight = exchanged(spread(kv_weight, ring), CHIP + ("zl",))
    pieces, halfway = team_pieces(*cut)
    weight, _ = lax.optimization_barrier((weight, halfway))
    weight_other = to_other_core(weight)
    part = exchanged(project(place, weight, weight_other, pieces, queries_in[0], out_grad[0]), "x")
    kv = summed(part, BF16)

    near, far = to_chip(kv, 1), to_chip(kv, 2)
    other = to_other_core(stacked(kv, near, far))
    attn, query_grad, grad_own, grad_other = attention(
        place, doc_lengths, queries_in[0], out_grad[0], kv, near, far, other
    )

    own_grad, near_grad, far_grad = homeward(place, grad_own, to_other_core(grad_other))
    far_grad, near_grad = to_chip(far_grad, -2), to_chip(near_grad, -1)
    team_grad = exchanged(gathered(own_grad, near_grad, far_grad, X), "x")
    theirs = to_other_core(weight_grad_parts(1, place, team_grad, pieces))
    ours = weight_grad_parts(0, place, team_grad, pieces)
    parts = exchanged(added(ours, theirs), ("yl", "zl"))
    weight_grad = summed(exchanged(summed(parts, BF16), ("zh", "yh")), F32)
    return attn[None], query_grad[None], weight_grad


def solution(mesh):
    fine = Mesh(mesh.devices.reshape(ZH, YH, YL, CORE, X, ZL), AXES)
    return jax.shard_map(
        per_device,
        mesh=fine,
        in_specs=(P(DP, CTX, None), P(DP, CTX, None), P(AXES, None), P(DP, CTX, None), P(DP, None)),
        out_specs=(P(DP, CTX, None), P(DP, CTX, None), P(AXES, None)),
        check_vma=False,
    )
```

```python
import functools

import jax
import jax.numpy as jnp
from jax import lax
from jax.experimental import pallas as pl
from jax.experimental.pallas import tpu as pltpu
from jax.sharding import Mesh, PartitionSpec as P

AXES = ("zh", "yh", "yl", "core", "x", "zl")
CTX = ("zh", "yh", "yl", "core")
CHIP = ("zh", "yh", "yl")
DP = ("x", "zl")
ZH, YH, YL, CORE, X, ZL = 4, 4, 2, 2, 4, 2
CHIPS = ZH * YH * YL
COUNT = 128
HEAD = 128
WIDTH = 2 * HEAD
BF16, F32 = jnp.bfloat16, jnp.float32
TOGETHER = 16
LOG2E = 1.4426950408889634
VMEM_LIMIT = 20 << 20
SMALL_LIMIT = 8 << 20


def vmem():
    return pl.BlockSpec(memory_space=pltpu.VMEM)


def smem():
    return pl.BlockSpec(memory_space=pltpu.SMEM)


def params(limit=VMEM_LIMIT):
    return pltpu.CompilerParams(vmem_limit_bytes=limit)


def small_call(kernel, *args, outs, name, places=0):
    return pl.pallas_call(
        kernel,
        in_specs=[smem()] * places + [vmem()] * (len(args) - places),
        out_specs=[vmem()] * len(outs),
        out_shape=[jax.ShapeDtypeStruct(shape, kind) for shape, kind in outs],
        compiler_params=params(SMALL_LIMIT),
        cost_estimate=pl.CostEstimate(flops=1 << 18, bytes_accessed=1 << 19, transcendentals=0),
        name=name,
    )(*args)


def exchanged(blocks, axes):
    return lax.all_to_all(blocks, axes, 0, 0, tiled=False)


def to_team(piece, step):
    return lax.ppermute(piece, "x", [(x, (x + step) % X) for x in range(X)])


def to_chip(block, hop):
    chips = range(CHIPS)
    return lax.ppermute(block, CHIP, [(i, i + hop) for i in chips if i + hop in chips])


def to_other_core(block):
    return lax.ppermute(block, "core", [(0, 1), (1, 0)])


def pieces_kernel(place, rows, own, ahead, behind, over, under, sorted_rows):
    core, x = place[0], place[1]
    span = 32 * X
    old = lax.broadcasted_iota(jnp.int32, (4 * span, 4 * span), 0)
    new = lax.broadcasted_iota(jnp.int32, (4 * span, 4 * span), 1)
    moved = (old // 32 % X) * span + (old // span) * 32 + old % 32
    turn = (new == moved).astype(F32).astype(BF16)
    for group in range(CHIPS // 4):
        for c in range(CORE):
            tiles = [rows[:, ((group * 4 + b) * CORE + c) * span :][:, :span] for b in range(4)]
            tile = jnp.dot(jnp.concatenate(tiles, axis=1), turn, preferred_element_type=F32).astype(BF16)
            for j in range(X):
                sorted_rows[c * X + j, :, group * span : (group + 1) * span] = tile[:, j * span : (j + 1) * span]
    for half in range(2):
        first = (core + half) % CORE * X
        own[half] = sorted_rows[first + x]
        ahead[half] = sorted_rows[first + (x + 1) % X]
        behind[half] = sorted_rows[first + (x + 3) % X]
        (over, under)[half][...] = sorted_rows[first + (x + 2) % X]


def make_pieces(place, rows):
    features = rows.shape[1] // (CORE * X)
    piece = (COUNT, features)
    return pl.pallas_call(
        pieces_kernel,
        in_specs=[smem(), vmem()],
        out_specs=[vmem()] * 5,
        out_shape=[jax.ShapeDtypeStruct(shape, BF16) for shape in [(2,) + piece] * 3 + [piece] * 2],
        scratch_shapes=[
            pltpu.VMEM((CORE * X,) + piece, BF16),
        ],
        compiler_params=params(),
        cost_estimate=pl.CostEstimate(flops=1 << 30, bytes_accessed=4 << 20, transcendentals=0),
        name="pieces",
    )(place, rows)


def team_pieces(own, ahead, behind, over, under):
    halfway = to_team(over, 1), to_team(under, -1)
    pieces = own, to_team(behind, -1), to_team(ahead, 1), to_team(halfway[0], 1), to_team(halfway[1], -1)
    return pieces, halfway


def halves(refs, half):
    own, after, before, over, under = refs
    return [(0, own[half]), (1, after[half]), (3, before[half]), (2, (over, under)[half][...])]


def project_kernel(place, weight, weight_other, own, after, before, over, under, early_q, early_g, out):
    del early_q, early_g
    refs = (own, after, before, over, under)
    rows = [w[...].reshape(CHIPS * 32, WIDTH) for w in (weight, weight_other)]
    for (step, first), (_, second) in zip(halves(refs, 0), halves(refs, 1)):
        part = jnp.dot(first, rows[0], preferred_element_type=F32)
        part += jnp.dot(second, rows[1], preferred_element_type=F32)
        out[(place[1] + step) % X] = part.astype(BF16)


def project(place, weight, weight_other, pieces, *early):
    return pl.pallas_call(
        project_kernel,
        in_specs=[smem()] + [vmem()] * 9,
        out_specs=vmem(),
        out_shape=jax.ShapeDtypeStruct((X, COUNT, WIDTH), BF16),
        compiler_params=params(),
        cost_estimate=pl.CostEstimate(flops=1 << 29, bytes_accessed=3 << 20, transcendentals=0),
        name="project",
    )(place, weight, weight_other, *pieces, *early)


def weight_grad_kernel(half, place, grads, own, after, before, over, under, out, total):
    turned, rows = [], []
    for step, piece in halves((own, after, before, over, under), half):
        turned.append(grads[(place[1] + step) % X].T)
        rows.append(piece)
    total[...] = jnp.dot(
        jnp.concatenate(turned, axis=1), jnp.concatenate(rows, axis=0), preferred_element_type=F32
    )
    for four in range(CHIPS // 4):
        block = total[:, four * 128 : four * 128 + 128].T.astype(BF16)
        for i in range(4):
            far, yl = divmod(four * 4 + i, YL)
            for zl in range(ZL):
                row = i * 32 + zl * 16
                out[yl * ZL + zl, far] = block[row : row + 16]


def weight_grad_parts(half, place, grads, pieces):
    features = pieces[0].shape[2]
    return pl.pallas_call(
        functools.partial(weight_grad_kernel, half),
        in_specs=[smem()] + [vmem()] * 6,
        out_specs=vmem(),
        out_shape=jax.ShapeDtypeStruct((YL * ZL, ZH * YH, 16, WIDTH), BF16),
        scratch_shapes=[pltpu.VMEM((WIDTH, features), F32)],
        compiler_params=params(),
        cost_estimate=pl.CostEstimate(flops=1 << 28, bytes_accessed=2 << 20, transcendentals=0),
        name="weight_grad",
    )(place, grads, *pieces)


def summed_kernel(parts, out):
    total = parts[0].astype(F32)
    for i in range(1, parts.shape[0]):
        total = total + parts[i].astype(F32)
    out[...] = total.astype(out.dtype)


def summed(parts, kind):
    return small_call(summed_kernel, parts, outs=[(parts.shape[1:], kind)], name="summed")[0]


def spread_kernel(block, out):
    for i in range(out.shape[0]):
        out[i] = block[...]


def spread(block, count):
    return small_call(spread_kernel, block, outs=[((count,) + block.shape, block.dtype)], name="spread")[0]


def stacked_kernel(*refs):
    for i, block in enumerate(refs[:-1]):
        refs[-1][i] = block[...]


def stacked(*blocks):
    shape = (len(blocks),) + blocks[0].shape
    return small_call(stacked_kernel, *blocks, outs=[(shape, blocks[0].dtype)], name="stacked")[0]


def added_kernel(one, other, out):
    out[...] = (one[...].astype(F32) + other[...].astype(F32)).astype(BF16)


def added(one, other):
    return small_call(added_kernel, one, other, outs=[(one.shape, BF16)], name="added")[0]


def homeward_kernel(place, own, back, total_own, near, far):
    first = place[0] == 0
    zero, one = back[0].astype(F32), back[1].astype(F32)
    total_own[...] = own[0] + jnp.where(first, zero, F32(0.0))
    near[...] = (own[1] + jnp.where(first, one, zero)).astype(BF16)
    far[...] = (own[2] + jnp.where(first, F32(0.0), one)).astype(BF16)


def homeward(place, own, back):
    block = own.shape[1:]
    outs = [(block, F32), (block, BF16), (block, BF16)]
    return small_call(homeward_kernel, place, own, back, outs=outs, name="homeward", places=1)


def gathered_kernel(own, near, far, out):
    total = (own[...] + near[...].astype(F32) + far[...].astype(F32)).astype(BF16)
    for i in range(out.shape[0]):
        out[i] = total


def gathered(own, near, far, count):
    return small_call(gathered_kernel, own, near, far, outs=[((count,) + own.shape, BF16)], name="gathered")[0]


def attention_kernel(place, lengths, queries, grads, own, near, far, other, attn, grad_q, grad_own, grad_other):
    core, chip_pos = place[0], place[2]
    scale = HEAD ** -0.5
    blocks = [own[...], near[...], far[...], other[1 - core], other[2 - core]]
    starts = [chip_pos + core * COUNT - 2 * COUNT * i for i in range(3)]
    starts += [chip_pos + (1 - core) * COUNT - 2 * COUNT * (1 - core + i) for i in range(2)]
    keys = jnp.concatenate([b[:, :HEAD] for b in blocks], axis=0)
    values = jnp.concatenate([b[:, HEAD:] for b in blocks], axis=0)
    keys_t, values_t = keys.T, values.T

    query_pos = starts[0] + lax.broadcasted_iota(jnp.int32, (1, COUNT), 1)
    doc_start = jnp.zeros((1, COUNT), jnp.int32)
    end = jnp.int32(0)
    for doc in range(lengths.shape[1]):
        end = end + lengths[0, doc]
        doc_start = jnp.where(query_pos >= end, end, doc_start)
    row = lax.broadcasted_iota(jnp.int32, (COUNT, COUNT), 0)
    masks = []
    for start in starts:
        key_pos = start + row
        masks.append((key_pos >= doc_start) & (key_pos <= query_pos))
    cap = jnp.where(jnp.concatenate(masks, axis=0), F32(jnp.inf), F32(-1e30))
    cap = jnp.concatenate([cap] * TOGETHER, axis=1)

    nt = (((1,), (1,)), ((), ()))
    total_k = total_v = None
    for turn in range(queries.shape[1] // (TOGETHER * HEAD)):
        cols = [slice(h * HEAD, (h + 1) * HEAD) for h in range(turn * TOGETHER, (turn + 1) * TOGETHER)]
        q = jnp.concatenate([queries[:, c] for c in cols], axis=0)
        g = jnp.concatenate([grads[:, c] for c in cols], axis=0)
        scores = lax.dot_general(keys, q, nt, preferred_element_type=F32) * F32(scale * LOG2E)
        scores = jnp.minimum(scores, cap)
        top = jnp.max(scores, axis=0, keepdims=True)
        weights = jnp.exp2(scores - top)
        inverse = 1.0 / jnp.sum(weights, axis=0, keepdims=True)
        dprobs = lax.dot_general(values, g, nt, preferred_element_type=F32)
        out_dot = jnp.sum(weights * dprobs, axis=0, keepdims=True) * inverse
        dscores = (weights * (dprobs - out_dot)).astype(BF16)
        weights = weights.astype(BF16)
        out = jnp.dot(values_t, weights, preferred_element_type=F32) * inverse
        dq = jnp.dot(keys_t, dscores, preferred_element_type=F32) * (inverse * scale)
        out, dq = out.T.astype(BF16), dq.T.astype(BF16)
        for i in range(TOGETHER):
            attn[:, cols[i]] = out[i * COUNT : (i + 1) * COUNT]
            grad_q[:, cols[i]] = dq[i * COUNT : (i + 1) * COUNT]
        column = jnp.broadcast_to(inverse, (HEAD, TOGETHER * HEAD)).T
        part_k = jnp.dot(dscores, (q.astype(F32) * column).astype(BF16), preferred_element_type=F32)
        part_v = jnp.dot(weights, (g.astype(F32) * column).astype(BF16), preferred_element_type=F32)
        total_k = part_k if turn == 0 else total_k + part_k
        total_v = part_v if turn == 0 else total_v + part_v
    total = jnp.concatenate([total_k * scale, total_v], axis=1)
    for i in range(3):
        grad_own[i] = total[i * COUNT : (i + 1) * COUNT]
    for i in range(2):
        grad_other[i] = total[(3 + i) * COUNT : (4 + i) * COUNT].astype(BF16)


def attention(place, lengths, queries, grads, own, near, far, other):
    shape = jax.ShapeDtypeStruct(queries.shape, BF16)
    return pl.pallas_call(
        attention_kernel,
        in_specs=[smem(), smem()] + [vmem()] * 6,
        out_specs=[vmem()] * 4,
        out_shape=[
            shape,
            shape,
            jax.ShapeDtypeStruct((3, COUNT, WIDTH), F32),
            jax.ShapeDtypeStruct((2, COUNT, WIDTH), BF16),
        ],
        compiler_params=params(),
        cost_estimate=pl.CostEstimate(flops=2 << 30, bytes_accessed=3 << 20, transcendentals=5 << 18),
        name="attention",
    )(place, lengths, queries, grads, own, near, far, other)


def per_device(tokens_in, queries_in, kv_weight, out_grad, doc_lengths):
    core, chip = lax.axis_index("core"), lax.axis_index(CHIP)
    place = jnp.stack([core, lax.axis_index("x"), chip * (CORE * COUNT)]).astype(jnp.int32)

    cut = make_pieces(place, tokens_in[0])
    ring = CHIPS * ZL
    weight = exchanged(spread(kv_weight, ring), CHIP + ("zl",))
    pieces, halfway = team_pieces(*cut)
    weight, _ = lax.optimization_barrier((weight, halfway[0]))
    weight_other = to_other_core(weight)
    part = exchanged(project(place, weight, weight_other, pieces, queries_in[0], out_grad[0]), "x")
    kv = summed(part, BF16)

    near, far = to_chip(kv, 1), to_chip(kv, 2)
    other = to_other_core(stacked(kv, near, far))
    attn, query_grad, grad_own, grad_other = attention(
        place, doc_lengths, queries_in[0], out_grad[0], kv, near, far, other
    )

    own_grad, near_grad, far_grad = homeward(place, grad_own, to_other_core(grad_other))
    far_grad, near_grad = to_chip(far_grad, -2), to_chip(near_grad, -1)
    team_grad = exchanged(gathered(own_grad, near_grad, far_grad, X), "x")
    theirs = to_other_core(weight_grad_parts(1, place, team_grad, pieces))
    ours = weight_grad_parts(0, place, team_grad, pieces)
    parts = exchanged(added(ours, theirs), ("yl", "zl"))
    weight_grad = summed(exchanged(summed(parts, BF16), ("zh", "yh")), F32)
    return attn[None], query_grad[None], weight_grad


def solution(mesh):
    fine = Mesh(mesh.devices.reshape(ZH, YH, YL, CORE, X, ZL), AXES)
    return jax.shard_map(
        per_device,
        mesh=fine,
        in_specs=(P(DP, CTX, None), P(DP, CTX, None), P(AXES, None), P(DP, CTX, None), P(DP, None)),
        out_specs=(P(DP, CTX, None), P(DP, CTX, None), P(AXES, None)),
        check_vma=False,
    )
```

```python
import functools

import jax
import jax.numpy as jnp
from jax import lax
from jax.experimental import pallas as pl
from jax.experimental.pallas import tpu as pltpu
from jax.sharding import Mesh, PartitionSpec as P

AXES = ("zh", "yh", "yl", "core", "x", "zl")
CTX = ("zh", "yh", "yl", "core")
CHIP = ("zh", "yh", "yl")
DP = ("x", "zl")
ZH, YH, YL, CORE, X, ZL = 4, 4, 2, 2, 4, 2
CHIPS = ZH * YH * YL
COUNT = 128
HEAD = 128
WIDTH = 2 * HEAD
BF16, F32 = jnp.bfloat16, jnp.float32
TOGETHER = 16
LOG2E = 1.4426950408889634
VMEM_LIMIT = 20 << 20
SMALL_LIMIT = 8 << 20


def vmem():
    return pl.BlockSpec(memory_space=pltpu.VMEM)


def smem():
    return pl.BlockSpec(memory_space=pltpu.SMEM)


def params(limit=VMEM_LIMIT):
    return pltpu.CompilerParams(vmem_limit_bytes=limit)


def small_call(kernel, *args, outs, name, places=0):
    return pl.pallas_call(
        kernel,
        in_specs=[smem()] * places + [vmem()] * (len(args) - places),
        out_specs=[vmem()] * len(outs),
        out_shape=[jax.ShapeDtypeStruct(shape, kind) for shape, kind in outs],
        compiler_params=params(SMALL_LIMIT),
        cost_estimate=pl.CostEstimate(flops=1 << 18, bytes_accessed=1 << 19, transcendentals=0),
        name=name,
    )(*args)


def exchanged(blocks, axes):
    return lax.all_to_all(blocks, axes, 0, 0, tiled=False)


def to_team(piece, step):
    return lax.ppermute(piece, "x", [(x, (x + step) % X) for x in range(X)])


def to_chip(block, hop):
    chips = range(CHIPS)
    return lax.ppermute(block, CHIP, [(i, i + hop) for i in chips if i + hop in chips])


def to_other_core(block):
    return lax.ppermute(block, "core", [(0, 1), (1, 0)])


def pieces_kernel(place, rows, own, ahead, behind, over, under, sorted_rows):
    core, x = place[0], place[1]
    span = 32 * X
    old = lax.broadcasted_iota(jnp.int32, (4 * span, 4 * span), 0)
    new = lax.broadcasted_iota(jnp.int32, (4 * span, 4 * span), 1)
    moved = (old // 32 % X) * span + (old // span) * 32 + old % 32
    turn = (new == moved).astype(F32).astype(BF16)
    for group in range(CHIPS // 4):
        for c in range(CORE):
            tiles = [rows[:, ((group * 4 + b) * CORE + c) * span :][:, :span] for b in range(4)]
            tile = jnp.dot(jnp.concatenate(tiles, axis=1), turn, preferred_element_type=F32).astype(BF16)
            for j in range(X):
                sorted_rows[c * X + j, :, group * span : (group + 1) * span] = tile[:, j * span : (j + 1) * span]
    for half in range(2):
        first = (core + half) % CORE * X
        own[half] = sorted_rows[first + x]
        ahead[half] = sorted_rows[first + (x + 1) % X]
        behind[half] = sorted_rows[first + (x + 3) % X]
        (over, under)[half][...] = sorted_rows[first + (x + 2) % X]


def make_pieces(place, rows):
    features = rows.shape[1] // (CORE * X)
    piece = (COUNT, features)
    return pl.pallas_call(
        pieces_kernel,
        in_specs=[smem(), vmem()],
        out_specs=[vmem()] * 5,
        out_shape=[jax.ShapeDtypeStruct(shape, BF16) for shape in [(2,) + piece] * 3 + [piece] * 2],
        scratch_shapes=[
            pltpu.VMEM((CORE * X,) + piece, BF16),
        ],
        compiler_params=params(),
        cost_estimate=pl.CostEstimate(flops=1 << 30, bytes_accessed=4 << 20, transcendentals=0),
        name="pieces",
    )(place, rows)


def team_pieces(own, ahead, behind, over, under):
    halfway = to_team(over, 1), to_team(under, -1)
    pieces = own, to_team(behind, -1), to_team(ahead, 1), to_team(halfway[0], 1), to_team(halfway[1], -1)
    return pieces, halfway


def halves(refs, half):
    own, after, before, over, under = refs
    return [(0, own[half]), (1, after[half]), (3, before[half]), (2, (over, under)[half][...])]


def projected(parts, weights):
    rows = [w[...].reshape(CHIPS * 32, WIDTH) for w in weights]
    total = jnp.dot(parts[0], rows[0], preferred_element_type=F32)
    return (total + jnp.dot(parts[1], rows[1], preferred_element_type=F32)).astype(BF16)


def project_kernel(place, weight, weight_other, own, after, before, early_q, early_g, out):
    del early_q, early_g
    for step, piece in ((0, own), (1, after), (3, before)):
        out[(place[1] + step) % X] = projected((piece[0], piece[1]), (weight, weight_other))


def project_last_kernel(place, weight, weight_other, over, under, parts, out):
    del parts
    out[(place[1] + 2) % X] = projected((over[...], under[...]), (weight, weight_other))


def project(place, weight, weight_other, pieces, *early):
    shape = jax.ShapeDtypeStruct((X, COUNT, WIDTH), BF16)
    parts = pl.pallas_call(
        project_kernel,
        in_specs=[smem()] + [vmem()] * 7,
        out_specs=vmem(),
        out_shape=shape,
        compiler_params=params(),
        cost_estimate=pl.CostEstimate(flops=3 << 27, bytes_accessed=3 << 20, transcendentals=0),
        name="project",
    )(place, weight, weight_other, *pieces[:3], *early)
    return pl.pallas_call(
        project_last_kernel,
        in_specs=[smem()] + [vmem()] * 5,
        out_specs=vmem(),
        out_shape=shape,
        input_output_aliases={5: 0},
        compiler_params=params(),
        cost_estimate=pl.CostEstimate(flops=1 << 27, bytes_accessed=1 << 20, transcendentals=0),
        name="project_last",
    )(place, weight, weight_other, *pieces[3:], parts)


def weight_grad_kernel(half, place, grads, own, after, before, over, under, out, total):
    turned, rows = [], []
    for step, piece in halves((own, after, before, over, under), half):
        turned.append(grads[(place[1] + step) % X].T)
        rows.append(piece)
    total[...] = jnp.dot(
        jnp.concatenate(turned, axis=1), jnp.concatenate(rows, axis=0), preferred_element_type=F32
    )
    for four in range(CHIPS // 4):
        block = total[:, four * 128 : four * 128 + 128].T.astype(BF16)
        for i in range(4):
            far, yl = divmod(four * 4 + i, YL)
            for zl in range(ZL):
                row = i * 32 + zl * 16
                out[yl * ZL + zl, far] = block[row : row + 16]


def weight_grad_parts(half, place, grads, pieces):
    features = pieces[0].shape[2]
    return pl.pallas_call(
        functools.partial(weight_grad_kernel, half),
        in_specs=[smem()] + [vmem()] * 6,
        out_specs=vmem(),
        out_shape=jax.ShapeDtypeStruct((YL * ZL, ZH * YH, 16, WIDTH), BF16),
        scratch_shapes=[pltpu.VMEM((WIDTH, features), F32)],
        compiler_params=params(),
        cost_estimate=pl.CostEstimate(flops=1 << 28, bytes_accessed=2 << 20, transcendentals=0),
        name="weight_grad",
    )(place, grads, *pieces)


def summed_kernel(parts, out):
    total = parts[0].astype(F32)
    for i in range(1, parts.shape[0]):
        total = total + parts[i].astype(F32)
    out[...] = total.astype(out.dtype)


def summed(parts, kind):
    return small_call(summed_kernel, parts, outs=[(parts.shape[1:], kind)], name="summed")[0]


def spread_kernel(block, out):
    for i in range(out.shape[0]):
        out[i] = block[...]


def spread(block, count):
    return small_call(spread_kernel, block, outs=[((count,) + block.shape, block.dtype)], name="spread")[0]


def stacked_kernel(*refs):
    for i, block in enumerate(refs[:-1]):
        refs[-1][i] = block[...]


def stacked(*blocks):
    shape = (len(blocks),) + blocks[0].shape
    return small_call(stacked_kernel, *blocks, outs=[(shape, blocks[0].dtype)], name="stacked")[0]


def added_kernel(one, other, out):
    out[...] = (one[...].astype(F32) + other[...].astype(F32)).astype(BF16)


def added(one, other):
    return small_call(added_kernel, one, other, outs=[(one.shape, BF16)], name="added")[0]


def homeward_kernel(place, own, back, total_own, near, far):
    first = place[0] == 0
    zero, one = back[0].astype(F32), back[1].astype(F32)
    total_own[...] = own[0] + jnp.where(first, zero, F32(0.0))
    near[...] = (own[1] + jnp.where(first, one, zero)).astype(BF16)
    far[...] = (own[2] + jnp.where(first, F32(0.0), one)).astype(BF16)


def homeward(place, own, back):
    block = own.shape[1:]
    outs = [(block, F32), (block, BF16), (block, BF16)]
    return small_call(homeward_kernel, place, own, back, outs=outs, name="homeward", places=1)


def gathered_kernel(own, near, far, out):
    total = (own[...] + near[...].astype(F32) + far[...].astype(F32)).astype(BF16)
    for i in range(out.shape[0]):
        out[i] = total


def gathered(own, near, far, count):
    return small_call(gathered_kernel, own, near, far, outs=[((count,) + own.shape, BF16)], name="gathered")[0]


def attention_kernel(place, lengths, queries, grads, own, near, far, other, attn, grad_q, grad_own, grad_other):
    core, chip_pos = place[0], place[2]
    scale = HEAD ** -0.5
    blocks = [own[...], near[...], far[...], other[1 - core], other[2 - core]]
    starts = [chip_pos + core * COUNT - 2 * COUNT * i for i in range(3)]
    starts += [chip_pos + (1 - core) * COUNT - 2 * COUNT * (1 - core + i) for i in range(2)]
    keys = jnp.concatenate([b[:, :HEAD] for b in blocks], axis=0)
    values = jnp.concatenate([b[:, HEAD:] for b in blocks], axis=0)
    keys_t, values_t = keys.T, values.T

    query_pos = starts[0] + lax.broadcasted_iota(jnp.int32, (1, COUNT), 1)
    doc_start = jnp.zeros((1, COUNT), jnp.int32)
    end = jnp.int32(0)
    for doc in range(lengths.shape[1]):
        end = end + lengths[0, doc]
        doc_start = jnp.where(query_pos >= end, end, doc_start)
    row = lax.broadcasted_iota(jnp.int32, (COUNT, COUNT), 0)
    masks = []
    for start in starts:
        key_pos = start + row
        masks.append((key_pos >= doc_start) & (key_pos <= query_pos))
    cap = jnp.where(jnp.concatenate(masks, axis=0), F32(jnp.inf), F32(-1e30))
    cap = jnp.concatenate([cap] * TOGETHER, axis=1)

    nt = (((1,), (1,)), ((), ()))
    total_k = total_v = None
    for turn in range(queries.shape[1] // (TOGETHER * HEAD)):
        cols = [slice(h * HEAD, (h + 1) * HEAD) for h in range(turn * TOGETHER, (turn + 1) * TOGETHER)]
        q = jnp.concatenate([queries[:, c] for c in cols], axis=0)
        g = jnp.concatenate([grads[:, c] for c in cols], axis=0)
        scores = lax.dot_general(keys, q, nt, preferred_element_type=F32) * F32(scale * LOG2E)
        scores = jnp.minimum(scores, cap)
        top = jnp.max(scores, axis=0, keepdims=True)
        weights = jnp.exp2(scores - top)
        inverse = 1.0 / jnp.sum(weights, axis=0, keepdims=True)
        dprobs = lax.dot_general(values, g, nt, preferred_element_type=F32)
        out_dot = jnp.sum(weights * dprobs, axis=0, keepdims=True) * inverse
        dscores = (weights * (dprobs - out_dot)).astype(BF16)
        weights = weights.astype(BF16)
        out = jnp.dot(values_t, weights, preferred_element_type=F32) * inverse
        dq = jnp.dot(keys_t, dscores, preferred_element_type=F32) * (inverse * scale)
        out, dq = out.T.astype(BF16), dq.T.astype(BF16)
        for i in range(TOGETHER):
            attn[:, cols[i]] = out[i * COUNT : (i + 1) * COUNT]
            grad_q[:, cols[i]] = dq[i * COUNT : (i + 1) * COUNT]
        column = jnp.broadcast_to(inverse, (HEAD, TOGETHER * HEAD)).T
        part_k = jnp.dot(dscores, (q.astype(F32) * column).astype(BF16), preferred_element_type=F32)
        part_v = jnp.dot(weights, (g.astype(F32) * column).astype(BF16), preferred_element_type=F32)
        total_k = part_k if turn == 0 else total_k + part_k
        total_v = part_v if turn == 0 else total_v + part_v
    total = jnp.concatenate([total_k * scale, total_v], axis=1)
    for i in range(3):
        grad_own[i] = total[i * COUNT : (i + 1) * COUNT]
    for i in range(2):
        grad_other[i] = total[(3 + i) * COUNT : (4 + i) * COUNT].astype(BF16)


def attention(place, lengths, queries, grads, own, near, far, other):
    shape = jax.ShapeDtypeStruct(queries.shape, BF16)
    return pl.pallas_call(
        attention_kernel,
        in_specs=[smem(), smem()] + [vmem()] * 6,
        out_specs=[vmem()] * 4,
        out_shape=[
            shape,
            shape,
            jax.ShapeDtypeStruct((3, COUNT, WIDTH), F32),
            jax.ShapeDtypeStruct((2, COUNT, WIDTH), BF16),
        ],
        compiler_params=params(),
        cost_estimate=pl.CostEstimate(flops=2 << 30, bytes_accessed=3 << 20, transcendentals=5 << 18),
        name="attention",
    )(place, lengths, queries, grads, own, near, far, other)


def per_device(tokens_in, queries_in, kv_weight, out_grad, doc_lengths):
    core, chip = lax.axis_index("core"), lax.axis_index(CHIP)
    place = jnp.stack([core, lax.axis_index("x"), chip * (CORE * COUNT)]).astype(jnp.int32)

    cut = make_pieces(place, tokens_in[0])
    ring = CHIPS * ZL
    weight = exchanged(spread(kv_weight, ring), CHIP + ("zl",))
    pieces, halfway = team_pieces(*cut)
    weight, _ = lax.optimization_barrier((weight, halfway[0]))
    weight_other = to_other_core(weight)
    part = exchanged(project(place, weight, weight_other, pieces, queries_in[0], out_grad[0]), "x")
    kv = summed(part, BF16)

    near, far = to_chip(kv, 1), to_chip(kv, 2)
    other = to_other_core(stacked(kv, near, far))
    attn, query_grad, grad_own, grad_other = attention(
        place, doc_lengths, queries_in[0], out_grad[0], kv, near, far, other
    )

    own_grad, near_grad, far_grad = homeward(place, grad_own, to_other_core(grad_other))
    far_grad, near_grad = to_chip(far_grad, -2), to_chip(near_grad, -1)
    team_grad = exchanged(gathered(own_grad, near_grad, far_grad, X), "x")
    theirs = to_other_core(weight_grad_parts(1, place, team_grad, pieces))
    ours = weight_grad_parts(0, place, team_grad, pieces)
    parts = exchanged(added(ours, theirs), ("yl", "zl"))
    weight_grad = summed(exchanged(summed(parts, BF16), ("zh", "yh")), F32)
    return attn[None], query_grad[None], weight_grad


def solution(mesh):
    fine = Mesh(mesh.devices.reshape(ZH, YH, YL, CORE, X, ZL), AXES)
    return jax.shard_map(
        per_device,
        mesh=fine,
        in_specs=(P(DP, CTX, None), P(DP, CTX, None), P(AXES, None), P(DP, CTX, None), P(DP, None)),
        out_specs=(P(DP, CTX, None), P(DP, CTX, None), P(AXES, None)),
        check_vma=False,
    )
```

```python
import functools

import jax
import jax.numpy as jnp
from jax import lax
from jax.experimental import pallas as pl
from jax.experimental.pallas import tpu as pltpu
from jax.sharding import Mesh, PartitionSpec as P

AXES = ("zh", "yh", "yl", "core", "x", "zl")
CTX = ("zh", "yh", "yl", "core")
CHIP = ("zh", "yh", "yl")
DP = ("x", "zl")
ZH, YH, YL, CORE, X, ZL = 4, 4, 2, 2, 4, 2
CHIPS = ZH * YH * YL
COUNT = 128
HEAD = 128
WIDTH = 2 * HEAD
BF16, F32 = jnp.bfloat16, jnp.float32
TOGETHER = 16
LOG2E = 1.4426950408889634
VMEM_LIMIT = 20 << 20
SMALL_LIMIT = 8 << 20


def vmem():
    return pl.BlockSpec(memory_space=pltpu.VMEM)


def smem():
    return pl.BlockSpec(memory_space=pltpu.SMEM)


def params(limit=VMEM_LIMIT):
    return pltpu.CompilerParams(vmem_limit_bytes=limit)


def small_call(kernel, *args, outs, name, places=0):
    return pl.pallas_call(
        kernel,
        in_specs=[smem()] * places + [vmem()] * (len(args) - places),
        out_specs=[vmem()] * len(outs),
        out_shape=[jax.ShapeDtypeStruct(shape, kind) for shape, kind in outs],
        compiler_params=params(SMALL_LIMIT),
        cost_estimate=pl.CostEstimate(flops=1 << 18, bytes_accessed=1 << 19, transcendentals=0),
        name=name,
    )(*args)


def exchanged(blocks, axes):
    return lax.all_to_all(blocks, axes, 0, 0, tiled=False)


def to_team(piece, step):
    return lax.ppermute(piece, "x", [(x, (x + step) % X) for x in range(X)])


def to_chip(block, hop):
    chips = range(CHIPS)
    return lax.ppermute(block, CHIP, [(i, i + hop) for i in chips if i + hop in chips])


def to_other_core(block):
    return lax.ppermute(block, "core", [(0, 1), (1, 0)])


def pieces_kernel(place, rows, own, ahead, behind, over, under, sorted_rows):
    core, x = place[0], place[1]
    span = 32 * X
    old = lax.broadcasted_iota(jnp.int32, (4 * span, 4 * span), 0)
    new = lax.broadcasted_iota(jnp.int32, (4 * span, 4 * span), 1)
    moved = (old // 32 % X) * span + (old // span) * 32 + old % 32
    turn = (new == moved).astype(F32).astype(BF16)
    for group in range(CHIPS // 4):
        for c in range(CORE):
            tiles = [rows[:, ((group * 4 + b) * CORE + c) * span :][:, :span] for b in range(4)]
            tile = jnp.dot(jnp.concatenate(tiles, axis=1), turn, preferred_element_type=F32).astype(BF16)
            for j in range(X):
                sorted_rows[c * X + j, :, group * span : (group + 1) * span] = tile[:, j * span : (j + 1) * span]
    for half in range(2):
        first = (core + half) % CORE * X
        own[half] = sorted_rows[first + x]
        ahead[half] = sorted_rows[first + (x + 1) % X]
        behind[half] = sorted_rows[first + (x + 3) % X]
        (over, under)[half][...] = sorted_rows[first + (x + 2) % X]


def make_pieces(place, rows):
    features = rows.shape[1] // (CORE * X)
    piece = (COUNT, features)
    return pl.pallas_call(
        pieces_kernel,
        in_specs=[smem(), vmem()],
        out_specs=[vmem()] * 5,
        out_shape=[jax.ShapeDtypeStruct(shape, BF16) for shape in [(2,) + piece] * 3 + [piece] * 2],
        scratch_shapes=[
            pltpu.VMEM((CORE * X,) + piece, BF16),
        ],
        compiler_params=params(),
        cost_estimate=pl.CostEstimate(flops=1 << 30, bytes_accessed=4 << 20, transcendentals=0),
        name="pieces",
    )(place, rows)


def team_pieces(own, ahead, behind, over, under):
    halfway = to_team(over, 1), to_team(under, -1)
    pieces = own, to_team(behind, -1), to_team(ahead, 1), to_team(halfway[0], 1), to_team(halfway[1], -1)
    return pieces, halfway


def halves(refs, half):
    own, after, before, over, under = refs
    return [(0, own[half]), (1, after[half]), (3, before[half]), (2, (over, under)[half][...])]


def projected(parts, weights):
    rows = [w[...].reshape(CHIPS * 32, WIDTH) for w in weights]
    total = jnp.dot(parts[0], rows[0], preferred_element_type=F32)
    return (total + jnp.dot(parts[1], rows[1], preferred_element_type=F32)).astype(BF16)


def project_kernel(place, weight, weight_other, own, after, before, early_q, early_g, out):
    del early_q, early_g
    for step, piece in ((0, own), (1, after), (3, before)):
        out[(place[1] + step) % X] = projected((piece[0], piece[1]), (weight, weight_other))


def project_last_kernel(place, weight, weight_other, over, under, parts, out):
    del parts
    out[(place[1] + 2) % X] = projected((over[...], under[...]), (weight, weight_other))


def project(place, weight, weight_other, pieces, *early):
    shape = jax.ShapeDtypeStruct((X, COUNT, WIDTH), BF16)
    parts = pl.pallas_call(
        project_kernel,
        in_specs=[smem()] + [vmem()] * 7,
        out_specs=vmem(),
        out_shape=shape,
        compiler_params=params(),
        cost_estimate=pl.CostEstimate(flops=3 << 27, bytes_accessed=3 << 20, transcendentals=0),
        name="project",
    )(place, weight, weight_other, *pieces[:3], *early)
    return pl.pallas_call(
        project_last_kernel,
        in_specs=[smem()] + [vmem()] * 5,
        out_specs=vmem(),
        out_shape=shape,
        input_output_aliases={5: 0},
        compiler_params=params(),
        cost_estimate=pl.CostEstimate(flops=1 << 27, bytes_accessed=1 << 20, transcendentals=0),
        name="project_last",
    )(place, weight, weight_other, *pieces[3:], parts)


def weight_grad_kernel(half, place, grads, own, after, before, over, under, out, total):
    turned, rows = [], []
    for step, piece in halves((own, after, before, over, under), half):
        turned.append(grads[(place[1] + step) % X].T)
        rows.append(piece)
    total[...] = jnp.dot(
        jnp.concatenate(turned, axis=1), jnp.concatenate(rows, axis=0), preferred_element_type=F32
    )
    for four in range(CHIPS // 4):
        block = total[:, four * 128 : four * 128 + 128].T.astype(BF16)
        for i in range(4):
            far, yl = divmod(four * 4 + i, YL)
            for zl in range(ZL):
                row = i * 32 + zl * 16
                out[yl * ZL + zl, far] = block[row : row + 16]


def weight_grad_parts(half, place, grads, pieces):
    features = pieces[0].shape[2]
    return pl.pallas_call(
        functools.partial(weight_grad_kernel, half),
        in_specs=[smem()] + [vmem()] * 6,
        out_specs=vmem(),
        out_shape=jax.ShapeDtypeStruct((YL * ZL, ZH * YH, 16, WIDTH), BF16),
        scratch_shapes=[pltpu.VMEM((WIDTH, features), F32)],
        compiler_params=params(),
        cost_estimate=pl.CostEstimate(flops=1 << 28, bytes_accessed=2 << 20, transcendentals=0),
        name="weight_grad",
    )(place, grads, *pieces)


def summed_kernel(parts, out):
    total = parts[0].astype(F32)
    for i in range(1, parts.shape[0]):
        total = total + parts[i].astype(F32)
    out[...] = total.astype(out.dtype)


def summed(parts, kind):
    return small_call(summed_kernel, parts, outs=[(parts.shape[1:], kind)], name="summed")[0]


def spread_kernel(block, out):
    for i in range(out.shape[0]):
        out[i] = block[...]


def spread(block, count):
    return small_call(spread_kernel, block, outs=[((count,) + block.shape, block.dtype)], name="spread")[0]


def stacked_kernel(*refs):
    for i, block in enumerate(refs[:-1]):
        refs[-1][i] = block[...]


def stacked(*blocks):
    shape = (len(blocks),) + blocks[0].shape
    return small_call(stacked_kernel, *blocks, outs=[(shape, blocks[0].dtype)], name="stacked")[0]


def added_kernel(one, other, out):
    out[...] = (one[...].astype(F32) + other[...].astype(F32)).astype(BF16)


def added(one, other):
    return small_call(added_kernel, one, other, outs=[(one.shape, BF16)], name="added")[0]


def homeward_kernel(place, own, back, total_own, near, far):
    first = place[0] == 0
    zero, one = back[0].astype(F32), back[1].astype(F32)
    total_own[...] = own[0] + jnp.where(first, zero, F32(0.0))
    near[...] = (own[1] + jnp.where(first, one, zero)).astype(BF16)
    far[...] = (own[2] + jnp.where(first, F32(0.0), one)).astype(BF16)


def homeward(place, own, back):
    block = own.shape[1:]
    outs = [(block, F32), (block, BF16), (block, BF16)]
    return small_call(homeward_kernel, place, own, back, outs=outs, name="homeward", places=1)


def gathered_kernel(own, near, far, out):
    total = (own[...] + near[...].astype(F32) + far[...].astype(F32)).astype(BF16)
    for i in range(out.shape[0]):
        out[i] = total


def gathered(own, near, far, count):
    return small_call(gathered_kernel, own, near, far, outs=[((count,) + own.shape, BF16)], name="gathered")[0]


def attention_kernel(place, lengths, queries, grads, own, near, far, other, attn, grad_q, grad_own, grad_other):
    core, chip_pos = place[0], place[2]
    scale = HEAD ** -0.5
    blocks = [own[...], near[...], far[...], other[1 - core], other[2 - core]]
    starts = [chip_pos + core * COUNT - 2 * COUNT * i for i in range(3)]
    starts += [chip_pos + (1 - core) * COUNT - 2 * COUNT * (1 - core + i) for i in range(2)]
    keys = jnp.concatenate([b[:, :HEAD] for b in blocks], axis=0)
    values = jnp.concatenate([b[:, HEAD:] for b in blocks], axis=0)
    keys_t, values_t = keys.T, values.T

    query_pos = starts[0] + lax.broadcasted_iota(jnp.int32, (1, COUNT), 1)
    doc_start = jnp.zeros((1, COUNT), jnp.int32)
    end = jnp.int32(0)
    for doc in range(lengths.shape[1]):
        end = end + lengths[0, doc]
        doc_start = jnp.where(query_pos >= end, end, doc_start)
    row = lax.broadcasted_iota(jnp.int32, (COUNT, COUNT), 0)
    masks = []
    for start in starts:
        key_pos = start + row
        masks.append((key_pos >= doc_start) & (key_pos <= query_pos))
    cap = jnp.where(jnp.concatenate(masks, axis=0), F32(jnp.inf), F32(-1e30))
    cap = jnp.concatenate([cap] * TOGETHER, axis=1)

    nt = (((1,), (1,)), ((), ()))
    total_k = total_v = None
    for turn in range(queries.shape[1] // (TOGETHER * HEAD)):
        cols = [slice(h * HEAD, (h + 1) * HEAD) for h in range(turn * TOGETHER, (turn + 1) * TOGETHER)]
        q = jnp.concatenate([queries[:, c] for c in cols], axis=0)
        g = jnp.concatenate([grads[:, c] for c in cols], axis=0)
        scores = lax.dot_general(keys, q, nt, preferred_element_type=F32) * F32(scale * LOG2E)
        scores = jnp.minimum(scores, cap)
        top = jnp.max(scores, axis=0, keepdims=True)
        weights = jnp.exp2(scores - top)
        inverse = 1.0 / jnp.sum(weights, axis=0, keepdims=True)
        dprobs = lax.dot_general(values, g, nt, preferred_element_type=F32)
        out_dot = jnp.sum(weights * dprobs, axis=0, keepdims=True) * inverse
        dscores = (weights * (dprobs - out_dot)).astype(BF16)
        weights = weights.astype(BF16)
        out = jnp.dot(values_t, weights, preferred_element_type=F32) * inverse
        dq = jnp.dot(keys_t, dscores, preferred_element_type=F32) * (inverse * scale)
        out, dq = out.T.astype(BF16), dq.T.astype(BF16)
        for i in range(TOGETHER):
            attn[:, cols[i]] = out[i * COUNT : (i + 1) * COUNT]
            grad_q[:, cols[i]] = dq[i * COUNT : (i + 1) * COUNT]
        column = jnp.broadcast_to(inverse, (HEAD, TOGETHER * HEAD)).T
        part_k = jnp.dot(dscores, (q.astype(F32) * column).astype(BF16), preferred_element_type=F32)
        part_v = jnp.dot(weights, (g.astype(F32) * column).astype(BF16), preferred_element_type=F32)
        total_k = part_k if turn == 0 else total_k + part_k
        total_v = part_v if turn == 0 else total_v + part_v
    total = jnp.concatenate([total_k * scale, total_v], axis=1)
    for i in range(3):
        grad_own[i] = total[i * COUNT : (i + 1) * COUNT]
    for i in range(2):
        grad_other[i] = total[(3 + i) * COUNT : (4 + i) * COUNT].astype(BF16)


def attention(place, lengths, queries, grads, own, near, far, other):
    shape = jax.ShapeDtypeStruct(queries.shape, BF16)
    return pl.pallas_call(
        attention_kernel,
        in_specs=[smem(), smem()] + [vmem()] * 6,
        out_specs=[vmem()] * 4,
        out_shape=[
            shape,
            shape,
            jax.ShapeDtypeStruct((3, COUNT, WIDTH), F32),
            jax.ShapeDtypeStruct((2, COUNT, WIDTH), BF16),
        ],
        compiler_params=params(),
        cost_estimate=pl.CostEstimate(flops=2 << 30, bytes_accessed=3 << 20, transcendentals=5 << 18),
        name="attention",
    )(place, lengths, queries, grads, own, near, far, other)


def per_device(tokens_in, queries_in, kv_weight, out_grad, doc_lengths):
    core, chip = lax.axis_index("core"), lax.axis_index(CHIP)
    place = jnp.stack([core, lax.axis_index("x"), chip * (CORE * COUNT)]).astype(jnp.int32)

    cut = make_pieces(place, tokens_in[0])
    ring = CHIPS * ZL
    weight = exchanged(spread(kv_weight, ring), CHIP + ("zl",))
    pieces, halfway = team_pieces(*cut)
    weight, _ = lax.optimization_barrier((weight, halfway))
    weight_other = to_other_core(weight)
    part = exchanged(project(place, weight, weight_other, pieces, queries_in[0], out_grad[0]), "x")
    kv = summed(part, BF16)

    near, far = to_chip(kv, 1), to_chip(kv, 2)
    other = to_other_core(stacked(kv, near, far))
    attn, query_grad, grad_own, grad_other = attention(
        place, doc_lengths, queries_in[0], out_grad[0], kv, near, far, other
    )

    own_grad, near_grad, far_grad = homeward(place, grad_own, to_other_core(grad_other))
    far_grad, near_grad = to_chip(far_grad, -2), to_chip(near_grad, -1)
    team_grad = exchanged(gathered(own_grad, near_grad, far_grad, X), "x")
    theirs = to_other_core(weight_grad_parts(1, place, team_grad, pieces))
    ours = weight_grad_parts(0, place, team_grad, pieces)
    parts = exchanged(added(ours, theirs), ("yl", "zl"))
    weight_grad = summed(exchanged(summed(parts, BF16), ("zh", "yh")), F32)
    return attn[None], query_grad[None], weight_grad


def solution(mesh):
    fine = Mesh(mesh.devices.reshape(ZH, YH, YL, CORE, X, ZL), AXES)
    return jax.shard_map(
        per_device,
        mesh=fine,
        in_specs=(P(DP, CTX, None), P(DP, CTX, None), P(AXES, None), P(DP, CTX, None), P(DP, None)),
        out_specs=(P(DP, CTX, None), P(DP, CTX, None), P(AXES, None)),
        check_vma=False,
    )
```
